256 devices in a mesh: seq: 32 (over y_hi, z, core), head: 8 (over x, y_lo).
Axes of the slice: x: 4, y: 4 (y_hi: 2, y_lo: 2; y = y_hi * 2 + y_lo), z: 8, core: 2. Of those that a mesh axis runs over, the one named last changes fastest.
Arguments:
- resid: bfloat16 [8192, 8192], P('seq'), may hold values from -6 to 6
- norm_gain: float32 [8192], replicated, may hold values from 0.1 to 1.9
- sender_diff: bfloat16 [8192, 4096], P('seq', 'head'), may hold values from -6 to 6
- w_out1: bfloat16 [4096, 8192], P('head', 'seq'), may hold values from -0.09375 to 0.09375
- w_query: bfloat16 [8192, 4096], P('seq', 'head')
- w_key: bfloat16 [8192, 1024], P('seq', 'head')
- w_value: bfloat16 [8192, 1024], P('seq', 'head'), may hold values from -0.0625 to 0.0625
- edge_mask: int32 [32, 32], replicated, may hold values 0 or 1
- doc_ids: int32 [32, 256], P('seq'), may hold values from 0 to 3, never falling along the last dimension, each value on 1 to 128 neighbouring positions
Outputs:
- patched: bfloat16 [8192, 4096], P('seq', 'head')
The draws below stay inside these ranges and needn't reach their ends.
All inputs are finite; a program needn't handle non-finite values.
Results may differ from the reference program's by a relative error of at most 0.0085.
The reference program's roundings to bfloat16 on the way count: a program that leaves them out, or rounds other values in their place, can miss the bound.
Values may be sent and summed in bfloat16 or wider, within the bound.
A program may use at most 128 MiB of HBM per device.

```python
import math
import jax
import jax.numpy as jnp
import numpy as np
from jax import lax

D = 8192
HEAD_SIZE = 128
KV = 8
SEND = 32
RH = 4
TOK_DEV = 256
RECV = 32
TOKENS = 8192
SHARDS = 32


def draw_pair(key):
    query_key = jax.random.fold_in(key, 11)
    noise_key = jax.random.fold_in(key, 12)
    query = jax.random.normal(query_key, (D, RECV * HEAD_SIZE), jnp.float32) * D ** (-0.5)
    noise = jax.random.normal(noise_key, (D, KV * HEAD_SIZE), jnp.float32) * D ** (-0.5)
    return (query, noise)


def draw_w_query(key, part):
    query, noise = draw_pair(key)
    return query.astype(jnp.bfloat16)


def draw_w_key(key, part):
    query, noise = draw_pair(key)
    return noise.astype(jnp.bfloat16)


def place_ends(array, rng, least, top_value):
    spot = [jax.random.randint(jax.random.fold_in(rng, axis), (), 0, length) for axis, length in enumerate(array.shape)]
    longest = array.shape.index(max(array.shape))
    beside = spot[:longest] + [(spot[longest] + 1) % array.shape[longest]] + spot[longest + 1:]
    return array.at[tuple(spot)].set(least).at[tuple(beside)].set(top_value)


def shard_levels(key, extent, pieces, low, top_value):
    loudness = 1.0
    for dim, shards_of in pieces:
        heights = jax.random.uniform(jax.random.fold_in(jax.random.fold_in(key, 6), dim), (shards_of,), jnp.float32, low / len(pieces), top_value / len(pieces))
        loudness = loudness * jnp.repeat(jnp.exp(heights), extent[dim] // shards_of).reshape((-1,) + (1,) * (len(extent) - 1 - dim))
    return loudness


def split_up(number_of, total, bound, lean):
    portions = [(1 << 20) // math.isqrt(grade ** lean) + 1 for grade in range(2, number_of + 1)]
    spare, holding = total - bound - (number_of - 1), [1] * (number_of - 1)
    while spare > 0:
        free = [i for i in range(number_of - 1) if holding[i] < bound]
        whole, remaining = sum([portions[i] for i in free]), spare
        for i in free:
            addition = min(bound - holding[i], max(1, remaining * portions[i] // whole), spare)
            holding[i] = holding[i] + addition
            spare = spare - addition
    return np.array([bound] + holding)


def ragged(rng, count, total, reach, skew):
    if count == 2:
        one = jax.random.randint(rng, (), max(1, total - reach), min(reach, total - 1) + 1)
        return jnp.stack([one, total - one])
    tallies = jnp.asarray(split_up(count, total, reach, skew), jnp.int32)
    pairs = (count - 1) // 2
    source_of, receiver = tallies[1:1 + 2 * pairs:2], tallies[2:2 + 2 * pairs:2]
    slack = jnp.minimum(source_of - 1, reach - receiver)
    passed = jax.random.randint(jax.random.fold_in(rng, 1), (pairs,), 0, 1 << 20) % (slack + 1)
    tallies = tallies.at[1:1 + 2 * pairs:2].set(source_of - passed).at[2:2 + 2 * pairs:2].set(receiver + passed)
    return tallies[jax.random.permutation(jax.random.fold_in(rng, 2), count)]


def scatter_about(rng, extent, scale, limit, pieces=(), held_as=jnp.bfloat16):
    factor_of = shard_levels(rng, extent, pieces, -0.22, 0.18) if pieces else 1.0
    result = jax.random.normal(rng, extent, jnp.float32) * scale * factor_of
    return jnp.minimum(jnp.maximum(result, -limit), limit).astype(held_as)


def setup_inputs(seed: int = 0) -> dict:
    seeds = jax.random.split(jax.random.key(seed), 10)
    return {
        "resid": scatter_about(seeds[0], (TOKENS, D), 1.0, 6.0, ((0, 32),)),
        "norm_gain": jnp.clip(1.0 + 0.18 * jax.random.normal(seeds[1], (D,), jnp.float32), 0.1, 1.9),
        "sender_diff": scatter_about(seeds[2], (TOKENS, SEND * HEAD_SIZE), 1.0, 6.0, ((0, 32), (1, 8))),
        "w_out1": scatter_about(seeds[3], (SEND * HEAD_SIZE, D), (SEND * HEAD_SIZE) ** -0.5, 0.09375, ((0, 8), (1, 32))),
        "w_query": draw_w_query(jax.random.fold_in(seeds[9], 71), 0),
        "w_key": draw_w_key(jax.random.fold_in(seeds[9], 71), 0),
        "w_value": scatter_about(seeds[6], (D, KV * HEAD_SIZE), D ** -0.5, 0.0625, ((0, 32), (1, 8))),
        "edge_mask": place_ends((jax.random.randint(seeds[7], (SEND, RECV), 0, 2) < 1).astype(jnp.int32), jax.random.fold_in(seeds[7], 1), 0, 1),
        "doc_ids": jax.vmap(lambda own: jnp.searchsorted(jnp.cumsum(ragged(own, 4, TOK_DEV, TOK_DEV // 2, 0)), jnp.arange(TOK_DEV), side="right"))(jax.random.split(seeds[8], SHARDS)).reshape((SHARDS, TOK_DEV)).astype(jnp.int32),
    }


epsilon = 1e-05

def attend(query, keys, values, doc_row):
    tokens = query.shape[0]
    query_head_rows = query.astype(jnp.float32).reshape(tokens, KV, RH, HEAD_SIZE)
    key_head_rows = keys.astype(jnp.float32).reshape(tokens, KV, HEAD_SIZE)
    value_head_rows = values.astype(jnp.float32).reshape(tokens, KV, HEAD_SIZE)
    attention_scores = jnp.einsum('pehm,qem->ehpq', query_head_rows, key_head_rows) * HEAD_SIZE ** (-0.5)
    position = jnp.arange(tokens, dtype=jnp.int32)
    allowed = (doc_row[:, None] == doc_row[None, :]) & (position[None, :] <= position[:, None])
    attention_scores = jnp.where(allowed, attention_scores, -jnp.inf)
    top = lax.optimization_barrier(jnp.max(attention_scores, axis=-1, keepdims=True))
    attention_weights = jnp.exp(attention_scores - top)
    attention_weights = (attention_weights / lax.optimization_barrier(jnp.sum(attention_weights, axis=-1, keepdims=True))).astype(jnp.bfloat16)
    mixed_values = jnp.einsum('uczp,puv->zucv', attention_weights.astype(jnp.float32), value_head_rows)
    return mixed_values.astype(jnp.bfloat16).reshape(tokens, RECV * HEAD_SIZE)

def reference(resid, norm_gain, sender_diff, w_out1, w_query, w_key, w_value, edge_mask, doc_ids):
    scaled = (w_query.astype(jnp.float32) * norm_gain[:, None]).astype(jnp.bfloat16)
    virtual = jnp.dot(w_out1, scaled, preferred_element_type=jnp.float32)
    mask = edge_mask.astype(jnp.float32)
    virtual = (virtual.reshape(SEND, HEAD_SIZE, RECV, HEAD_SIZE) * mask[:, None, :, None]).reshape(SEND * HEAD_SIZE, RECV * HEAD_SIZE)
    virtual = virtual.astype(jnp.bfloat16)

    def shard(inputs):
        resid_part, diff_part, doc_row = inputs
        resid_wide = resid_part.astype(jnp.float32)
        inv_rms = lax.rsqrt(lax.optimization_barrier(jnp.mean(resid_wide * resid_wide, axis=1)) + epsilon)
        normed = (resid_wide * inv_rms[:, None] * norm_gain[None, :]).astype(jnp.bfloat16)
        clean_query = jnp.dot(normed, w_query, preferred_element_type=jnp.float32)
        keys = jnp.dot(normed, w_key, preferred_element_type=jnp.float32).astype(jnp.bfloat16)
        values = jnp.dot(normed, w_value, preferred_element_type=jnp.float32).astype(jnp.bfloat16)
        delta = jnp.dot(diff_part, virtual, preferred_element_type=jnp.float32)
        query = (clean_query + inv_rms[:, None] * delta).astype(jnp.bfloat16)
        return attend(query, keys, values, doc_row)
    patched = lax.map(shard, (resid.reshape(SHARDS, TOK_DEV, D), sender_diff.reshape(SHARDS, TOK_DEV, SEND * HEAD_SIZE), doc_ids))
    return patched.reshape(TOKENS, RECV * HEAD_SIZE)
```

```python
import jax
import jax.numpy as jnp
from jax import lax
from jax.experimental import pallas as pl
from jax.experimental.pallas import tpu as pltpu
from jax.sharding import PartitionSpec as P

HEAD_SIZE = 128
epsilon = 1e-05
NZ = 8
MESH = pl.DeviceIdType.MESH


def rem(a, n):
    return lax.rem(a, n)


def kernel(
    resid_hbm, gain_ref, gain_cols_ref, sender_hbm, out1_hbm, wq_hbm, wk_hbm, wv_hbm,
    edge_ref, doc_row_ref, doc_col_ref,
    out_ref,
    resid, w_all, v_all, s_all, wo, wo_own, wo_mid, acc, acc_v, inv_ref,
    local_sem, w_recv, w_half, w_send, v_recv, v_half, v_send,
    s_recv, s_send, a_recv, a_send, b_recv, b_send, c_recv, c_send,
):
    me = lax.axis_index("seq")
    head = lax.axis_index("head")
    y = me // 16
    z = rem(me // 2, NZ)
    c = rem(me, 2)
    oy, oc = 1 - y, 1 - c

    def seq_of(yy, zz, cc):
        return yy * 16 + zz * 2 + cc

    loads = [
        pltpu.make_async_copy(out1_hbm, wo_own, local_sem.at[0]),
        pltpu.make_async_copy(wq_hbm, w_all.at[y, z, c, :, pl.ds(0, 512)], local_sem.at[1]),
        pltpu.make_async_copy(wk_hbm, w_all.at[y, z, c, :, pl.ds(512, 128)], local_sem.at[2]),
        pltpu.make_async_copy(wv_hbm, w_all.at[y, z, c, :, pl.ds(640, 128)], local_sem.at[3]),
        pltpu.make_async_copy(resid_hbm, resid, local_sem.at[4]),
        pltpu.make_async_copy(sender_hbm, s_all.at[head], local_sem.at[5]),
    ]
    for load in loads:
        load.start()

    barrier = pltpu.get_barrier_semaphore()

    def greet_seq(o, _):
        pl.semaphore_signal(
            barrier, inc=1, device_id=(rem(me + o, 32), head), device_id_type=MESH
        )
        return 0

    def greet_head(o, _):
        pl.semaphore_signal(
            barrier, inc=1, device_id=(me, rem(head + o, 8)), device_id_type=MESH
        )
        return 0

    lax.fori_loop(1, 8, greet_head, 0)
    lax.fori_loop(1, 32, greet_seq, 0)
    loads[0].wait()
    pl.semaphore_wait(barrier, 38)

    def a_copy(o):
        peer = rem(head + o, 8)
        return pltpu.make_async_remote_copy(
            src_ref=wo_own.at[:, peer], dst_ref=wo_mid.at[head],
            send_sem=a_send.at[o], recv_sem=a_recv.at[head],
            device_id=(me, peer), device_id_type=MESH,
        )

    def a_arrival(o):
        peer = rem(head + o, 8)
        return pltpu.make_async_remote_copy(
            src_ref=wo_own.at[:, peer], dst_ref=wo_mid.at[peer],
            send_sem=a_send.at[o], recv_sem=a_recv.at[peer],
            device_id=(me, peer), device_id_type=MESH,
        )

    a_local = pltpu.make_async_copy(wo_own.at[:, head], wo_mid.at[head], local_sem.at[6])

    def loop(n, f):
        def body(o, _):
            f(o)
            return 0

        lax.fori_loop(1, n, body, 0)

    loop(8, lambda o: a_copy(o).start())
    a_local.start()

    class Ring:
        def __init__(self, buf, recv, half, send):
            self.buf, self.recv, self.half, self.send = buf, recv, half, send
            self.rows = buf.shape[3] // 2
            self.sent = []

        def desc(self, slot, target, part=None, recv=None, index=0):
            view = self.buf.at[slot]
            if part is not None:
                view = self.buf.at[slot[0], slot[1], slot[2], pl.ds(part * self.rows, self.rows)]
            if recv is None:
                recv = self.recv.at[seq_of(*slot)]
            return pltpu.make_async_remote_copy(
                src_ref=view, dst_ref=view, send_sem=self.send.at[index], recv_sem=recv,
                device_id=(target, head), device_id_type=MESH,
            )

        def put(self, slot, target, part=None, recv=None):
            copy = self.desc(slot, target, part, recv, len(self.sent))
            copy.start()
            self.sent.append(copy)

        def got(self, slot, part=None, recv=None):
            self.desc(slot, seq_of(y, z, oc), part, recv).wait_recv()

        def spread(self, slot, across):
            if across:
                self.put(slot, seq_of(oy, z, c))
            for step in (1, NZ - 1):
                self.put(slot, seq_of(y, rem(z + step, NZ), c))
            self.put(slot, seq_of(y, z, oc))

        def across(self):
            slot = (oy, z, c)
            self.got(slot)
            self.spread(slot, False)
            self.got((oy, z, oc))
            return [(oy, z)]

        def own(self):
            self.got((y, z, oc))
            return [(y, z)]

        def plane(self, yy, d):
            if d == 4:
                zz = rem(z + 4, NZ)
                slot = (yy, zz, c)
                self.got(slot, 0)
                self.got(slot, 1, self.half.at[yy])
                self.put(slot, seq_of(y, z, oc))
                self.got((yy, zz, oc))
                return [(yy, zz)]
            chips = []
            for part, step in ((0, 1), (1, NZ - 1)):
                zz = rem(z + (NZ - step) * d, NZ)
                slot = (yy, zz, c)
                self.got(slot)
                onward = seq_of(y, rem(z + step, NZ), c)
                if d < 3:
                    self.put(slot, onward)
                elif part == 0:
                    self.put(slot, onward, 0)
                else:
                    self.put(slot, onward, 1, self.half.at[yy])
                self.put(slot, seq_of(y, z, oc))
                chips.append((yy, zz))
            for yy, zz in chips:
                self.got((yy, zz, oc))
            return chips

        def finish(self):
            for copy in self.sent:
                copy.wait_send()

    ring = Ring(w_all, w_recv, w_half, w_send)
    for load in loads[1:4]:
        load.wait()
    ring.spread((y, z, c), True)

    loads[4].wait()

    def add_squares(k, total):
        part = resid[:, pl.ds(pl.multiple_of(k * 512, 512), 512)].astype(jnp.float32)
        part = part * part
        return total + part[:, :128] + part[:, 128:256] + part[:, 256:384] + part[:, 384:]

    squares = lax.fori_loop(0, 16, add_squares, jnp.zeros((256, 128), jnp.float32))
    inv_ref[...] = lax.rsqrt(jnp.sum(squares, axis=1, keepdims=True) * (1.0 / 8192) + epsilon)

    loop(8, lambda o: a_arrival(o).wait_recv())
    a_local.wait()

    def b_copy(o):
        peer = rem(me + o, 32)
        return pltpu.make_async_remote_copy(
            src_ref=wo_mid.at[peer // 4, rem(peer, 4)], dst_ref=wo.at[head, me],
            send_sem=b_send.at[o], recv_sem=b_recv.at[me],
            device_id=(peer, head), device_id_type=MESH,
        )

    def b_arrival(o):
        peer = rem(me + o, 32)
        return pltpu.make_async_remote_copy(
            src_ref=wo_mid.at[peer // 4, rem(peer, 4)], dst_ref=wo.at[head, peer],
            send_sem=b_send.at[o], recv_sem=b_recv.at[peer],
            device_id=(peer, head), device_id_type=MESH,
        )

    b_local = pltpu.make_async_copy(
        wo_mid.at[me // 4, rem(me, 4)], wo.at[head, me], local_sem.at[7]
    )
    loop(32, lambda o: b_copy(o).start())
    b_local.start()

    acc[...] = jnp.zeros_like(acc)
    acc_v[...] = jnp.zeros_like(acc_v)

    def project(chips):
        for yy, zz in chips:
            at = pl.multiple_of((yy * 8 + zz) * 512, 512)
            part = resid[:, pl.ds(at, 512)].astype(jnp.float32)
            normed = (part * inv_ref[...] * gain_ref[:, pl.ds(at, 512)]).astype(jnp.bfloat16)
            acc[...] += jnp.dot(
                normed, w_all[yy, zz].reshape(512, 768), preferred_element_type=jnp.float32
            )

    lane = lax.broadcasted_iota(jnp.int32, (256, 32), 1)

    def virtual_part(chips):
        for yy, zz in chips:
            for cc in range(2):
                j = seq_of(yy, zz, cc)
                gain = jnp.sum(
                    jnp.where(lane == j, gain_cols_ref[...], 0.0), axis=1, keepdims=True
                )
                scaled = (
                    w_all[yy, zz, cc, :, :512].astype(jnp.float32) * gain
                ).astype(jnp.bfloat16)
                acc_v[...] += jnp.dot(
                    wo[:, j].reshape(128, 256), scaled, preferred_element_type=jnp.float32
                )

    waiting = []

    def take(chips):
        project(chips)
        waiting.extend(chips)

    take(ring.own())
    take(ring.plane(y, 1))

    loop(32, lambda o: b_arrival(o).wait_recv())
    b_local.wait()

    def gather_copy(buf, send, recv, o, arriving):
        peer = rem(head + o, 8)
        slot = peer if arriving else head
        return pltpu.make_async_remote_copy(
            src_ref=buf.at[slot], dst_ref=buf.at[slot],
            send_sem=send.at[o], recv_sem=recv.at[slot],
            device_id=(me, peer), device_id_type=MESH,
        )

    loop(8, lambda o: gather_copy(wo, c_send, c_recv, o, False).start())
    loads[5].wait()
    loop(8, lambda o: gather_copy(s_all, s_send, s_recv, o, False).start())

    take(ring.across())
    take(ring.plane(y, 2))
    take(ring.plane(oy, 1))
    take(ring.plane(y, 3))
    take(ring.plane(oy, 2))
    take(ring.plane(y, 4))
    loop(8, lambda o: gather_copy(wo, c_send, c_recv, o, True).wait_recv())
    virtual_part(waiting)
    for chips in (ring.plane(oy, 3), ring.plane(oy, 4)):
        project(chips)
        virtual_part(chips)

    for r in range(4):
        cols = pl.ds(r * 128, 128)
        keep = edge_ref[me, head * 4 + r].astype(jnp.float32)
        v_all[y, z, c, :, cols] = (acc_v[:, cols] * keep).astype(jnp.bfloat16)
    vring = Ring(v_all, v_recv, v_half, v_send)
    vring.spread((y, z, c), True)

    loop(8, lambda o: gather_copy(s_all, s_send, s_recv, o, True).wait_recv())

    def patch(chips):
        for yy, zz in chips:
            k = yy * 8 + zz
            rows = s_all[k // 2, :, pl.ds(pl.multiple_of(rem(k, 2) * 256, 256), 256)]
            acc[:, :512] += inv_ref[...] * jnp.dot(
                rows, v_all[yy, zz].reshape(256, 512), preferred_element_type=jnp.float32
            )

    keys = acc[:, 512:640].astype(jnp.bfloat16)
    values = acc[:, 640:768].astype(jnp.bfloat16)

    patch(vring.own())
    patch(vring.plane(y, 1))
    patch(vring.across())
    patch(vring.plane(y, 2))
    patch(vring.plane(oy, 1))
    patch(vring.plane(y, 3))
    patch(vring.plane(oy, 2))
    patch(vring.plane(y, 4))
    patch(vring.plane(oy, 3))
    patch(vring.plane(oy, 4))

    row = lax.broadcasted_iota(jnp.int32, (256, 256), 0)
    col = lax.broadcasted_iota(jnp.int32, (256, 256), 1)
    allowed = (doc_col_ref[...] == doc_row_ref[...]) & (col <= row)
    for r in range(4):
        cols = pl.ds(r * 128, 128)
        query = acc[:, cols].astype(jnp.bfloat16)
        scores = lax.dot_general(
            query, keys, (((1,), (1,)), ((), ())), preferred_element_type=jnp.float32
        ) * HEAD_SIZE ** (-0.5)
        scores = jnp.where(allowed, scores, -jnp.inf)
        weights = jnp.exp(scores - jnp.max(scores, axis=1, keepdims=True))
        weights = (weights / jnp.sum(weights, axis=1, keepdims=True)).astype(jnp.bfloat16)
        out_ref[:, cols] = jnp.dot(
            weights, values, preferred_element_type=jnp.float32
        ).astype(jnp.bfloat16)

    ring.finish()
    vring.finish()
    loop(8, lambda o: a_copy(o).wait_send())
    loop(32, lambda o: b_copy(o).wait_send())
    loop(8, lambda o: gather_copy(wo, c_send, c_recv, o, False).wait_send())
    loop(8, lambda o: gather_copy(s_all, s_send, s_recv, o, False).wait_send())


def local(resid, norm_gain, sender_diff, w_out1, w_query, w_key, w_value, edge_mask, doc_ids):
    dma = pltpu.SemaphoreType.DMA
    anywhere = pl.BlockSpec(memory_space=pl.ANY)
    vmem = pl.BlockSpec(memory_space=pltpu.VMEM)
    smem = pl.BlockSpec(memory_space=pltpu.SMEM)
    bf16, f32 = jnp.bfloat16, jnp.float32
    return pl.pallas_call(
        kernel,
        out_shape=jax.ShapeDtypeStruct((256, 512), bf16),
        in_specs=[
            anywhere, vmem, vmem, anywhere, anywhere, anywhere, anywhere, anywhere,
            smem, vmem, vmem,
        ],
        out_specs=vmem,
        scratch_shapes=[
            pltpu.VMEM((256, 8192), bf16),
            pltpu.VMEM((2, NZ, 2, 256, 768), bf16),
            pltpu.VMEM((2, NZ, 2, 128, 512), bf16),
            pltpu.VMEM((8, 256, 512), bf16),
            pltpu.VMEM((8, 32, 16, 256), bf16),
            pltpu.VMEM((4, 8, 16, 256), bf16),
            pltpu.VMEM((8, 4, 16, 256), bf16),
            pltpu.VMEM((256, 768), f32),
            pltpu.VMEM((128, 512), f32),
            pltpu.VMEM((256, 1), f32),
            dma((8,)),
            dma((32,)), dma((2,)), dma((40,)),
            dma((32,)), dma((2,)), dma((40,)),
            dma((8,)), dma((8,)),
            dma((8,)), dma((8,)),
            dma((32,)), dma((32,)),
            dma((8,)), dma((8,)),
        ],
        compiler_params=pltpu.CompilerParams(
            collective_id=0, has_side_effects=True, vmem_limit_bytes=60 * 1024 * 1024
        ),
        name="patch_layer",
    )(
        resid,
        norm_gain.reshape(1, -1),
        norm_gain.reshape(32, 256).T,
        sender_diff,
        w_out1.reshape(4, 8, 16, 256),
        w_query,
        w_key,
        w_value,
        edge_mask,
        doc_ids,
        doc_ids.reshape(-1, 1),
    )


def solution(mesh):
    placed = (
        P("seq", None),
        P(),
        P("seq", "head"),
        P("head", "seq"),
        P("seq", "head"),
        P("seq", "head"),
        P("seq", "head"),
        P(),
        P("seq", None),
    )
    return jax.shard_map(
        local, mesh=mesh, in_specs=placed, out_specs=P("seq", "head"), check_vma=False
    )
```

```python
import jax
import jax.numpy as jnp
from jax import lax
from jax.experimental import pallas as pl
from jax.experimental.pallas import tpu as pltpu
from jax.sharding import PartitionSpec as P

HEAD_SIZE = 128
epsilon = 1e-05
NZ = 8
MESH = pl.DeviceIdType.MESH


def rem(a, n):
    return lax.rem(a, n)


def kernel(
    resid_hbm, gain_ref, sender_hbm, out1_hbm, wq_hbm, wk_hbm, wv_hbm, edge_ref, doc_ref,
    out_ref,
    resid, q_all, kv_all, v_all, s_all, wo, wo_own, wo_mid, acc, acc_kv, acc_v, inv_ref,
    local_sem, token_sem, q_sems, kv_sems, v_sems, wo_sems, s_sems,
    a_recv, a_send, b_recv, b_send,
):
    me = lax.axis_index("seq")
    head = lax.axis_index("head")
    y = me // 16
    z = rem(me // 2, NZ)
    c = rem(me, 2)
    oy, oc = 1 - y, 1 - c
    x = head // 2
    low = rem(head, 2)
    olow = 1 - low

    def seq_of(yy, zz, cc):
        return yy * 16 + zz * 2 + cc

    def at_z(step):
        return rem(z + (step + NZ), NZ)

    def at_x(step):
        return rem(x + (step + 4), 4)

    loads = [
        pltpu.make_async_copy(out1_hbm, wo_own, local_sem.at[0]),
        pltpu.make_async_copy(wq_hbm, q_all.at[y, z, c], local_sem.at[1]),
        pltpu.make_async_copy(wk_hbm, kv_all.at[y, z, c, :, pl.ds(0, 128)], local_sem.at[2]),
        pltpu.make_async_copy(wv_hbm, kv_all.at[y, z, c, :, pl.ds(128, 128)], local_sem.at[3]),
        pltpu.make_async_copy(resid_hbm, resid, local_sem.at[4]),
        pltpu.make_async_copy(sender_hbm, s_all.at[head], local_sem.at[5]),
    ]
    for k in (1, 0, 2, 3, 4, 5):
        loads[k].start()

    def loop(n, f):
        def body(o, _):
            f(o)
            return 0

        lax.fori_loop(1, n, body, 0)

    def tell(sem, device):
        pl.semaphore_signal(sem, inc=1, device_id=device, device_id_type=MESH)

    barrier = pltpu.get_barrier_semaphore()
    across_dev = (seq_of(oy, z, c), head)
    core_dev = (seq_of(y, z, oc), head)
    up_dev = (seq_of(y, at_z(1), c), head)
    down_dev = (seq_of(y, at_z(-1), c), head)
    for device in (across_dev, up_dev, down_dev, core_dev):
        tell(barrier, device)
    loop(8, lambda o: tell(barrier, (me, rem(head + o, 8))))
    loads[1].wait()
    loads[0].wait()
    pl.semaphore_wait(barrier, 11)

    class Ring:
        def __init__(self, buf, sems, first):
            self.buf = buf
            self.recv, self.recv_b, self.half, self.send = sems
            self.rows = buf.shape[3]
            self.first = first
            self.whole = (0, self.rows)
            self.a = (0, first)
            self.b = (first, self.rows - first)
            self.sent = []

        def desc(self, slot, rows, device, recv, index=0):
            view = self.buf.at[slot[0], slot[1], slot[2], pl.ds(*rows)]
            return pltpu.make_async_remote_copy(
                src_ref=view, dst_ref=view, send_sem=self.send.at[index], recv_sem=recv,
                device_id=device, device_id_type=MESH,
            )

        def put(self, slot, rows, device, recv):
            copy = self.desc(slot, rows, device, recv, len(self.sent))
            copy.start()
            self.sent.append(copy)

        def got(self, slot, rows, recv):
            self.desc(slot, rows, core_dev, recv).wait_recv()

        def main(self, slot):
            return self.recv.at[seq_of(*slot)]

        def late(self, slot):
            return self.recv_b.at[seq_of(*slot)]

        def start(self):
            slot = (y, z, c)
            self.put(slot, self.whole, up_dev, self.main(slot))
            self.put(slot, self.whole, down_dev, self.main(slot))
            self.put(slot, self.a, across_dev, self.main(slot))
            self.put(slot, self.whole, core_dev, self.main(slot))
            self.put(slot, self.b, across_dev, self.late(slot))

        def round(self, yy, d, rows, kind):
            cut = (rows[0], rows[1] // 2), (rows[0] + rows[1] // 2, rows[1] // 2)
            if d == 4:
                slot = (yy, at_z(4), c)
                self.got(slot, cut[0], self.main(slot))
                self.got(slot, cut[1], self.half.at[kind])
                arrived = [slot]
            else:
                arrived = []
                for part, step, onward in ((0, 1, up_dev), (1, -1, down_dev)):
                    slot = (yy, at_z(-step * d), c)
                    self.got(slot, rows, self.main(slot))
                    if d < 3:
                        self.put(slot, rows, onward, self.main(slot))
                    else:
                        recv = self.half.at[kind] if part else self.main(slot)
                        self.put(slot, cut[part], onward, recv)
                    arrived.append(slot)
            for slot in arrived:
                if kind == 0:
                    self.put(slot, self.b, across_dev, self.late(slot))
                self.put(slot, rows, core_dev, self.main(slot))

        def plane(self, d):
            self.round(y, d, self.whole, 0)

        def other(self, d):
            self.round(oy, d, self.a, 1)

        def other_start(self):
            slot = (oy, z, c)
            self.got(slot, self.a, self.main(slot))
            self.put(slot, self.a, up_dev, self.main(slot))
            self.put(slot, self.a, down_dev, self.main(slot))
            self.put(slot, self.a, core_dev, self.main(slot))

        def places(self, d):
            return [at_z(d)] if d in (0, 4) else [at_z(-d), at_z(d)]

        def cross(self, d):
            for zz in self.places(d):
                slot = (oy, zz, c)
                self.got(slot, self.b, self.late(slot))
                self.put(slot, self.b, core_dev, self.late(slot))

        def chips(self, d):
            for zz in self.places(d):
                slot = (y, zz, oc)
                self.got(slot, self.whole, self.main(slot))
            return [(y, zz) for zz in self.places(d)]

        def other_chips(self, d):
            for zz in self.places(d):
                slot = (oy, zz, oc)
                self.got(slot, self.a, self.main(slot))
                self.got(slot, self.b, self.late(slot))
            return [(oy, zz) for zz in self.places(d)]

        def finish(self):
            for copy in self.sent:
                copy.wait_send()

    class HeadRing:
        def __init__(self, buf, sems):
            self.buf = buf
            self.recv, self.half, self.send = sems
            self.size = buf.shape[1]
            self.sent = []

        def desc(self, slot, rows, device, recv, index=0):
            view = self.buf.at[slot, pl.ds(*rows)]
            return pltpu.make_async_remote_copy(
                src_ref=view, dst_ref=view, send_sem=self.send.at[index], recv_sem=recv,
                device_id=device, device_id_type=MESH,
            )

        def put(self, slot, rows, step, recv, swap=False):
            device = (me, x * 2 + olow) if swap else (me, at_x(step) * 2 + low)
            copy = self.desc(slot, rows, device, recv, len(self.sent))
            copy.start()
            self.sent.append(copy)

        def got(self, slot, rows, recv):
            self.desc(slot, rows, (me, x * 2 + olow), recv).wait_recv()

        def start(self):
            whole = (0, self.size)
            for step in (1, -1):
                self.put(head, whole, step, self.recv.at[head])
            self.put(head, whole, 0, self.recv.at[head], swap=True)

        def pair(self):
            whole, slot = (0, self.size), x * 2 + olow
            self.got(slot, whole, self.recv.at[slot])
            for step in (1, -1):
                self.put(slot, whole, step, self.recv.at[slot])

        def one(self, kind):
            half = self.size // 2
            ll = olow if kind else low
            for part, step in ((0, 1), (1, -1)):
                slot = at_x(-step) * 2 + ll
                self.got(slot, (0, self.size), self.recv.at[slot])
                recv = self.half.at[kind] if part else self.recv.at[slot]
                self.put(slot, (part * half, half), step, recv)

        def two(self, kind):
            half = self.size // 2
            slot = at_x(2) * 2 + (olow if kind else low)
            self.got(slot, (0, half), self.recv.at[slot])
            self.got(slot, (half, half), self.half.at[kind])

        def finish(self):
            for copy in self.sent:
                copy.wait_send()

    qring = Ring(q_all, q_sems, 128)
    kvring = Ring(kv_all, kv_sems, 128)
    vring = Ring(v_all, v_sems, 64)
    oring = HeadRing(wo, wo_sems)
    sring = HeadRing(s_all, s_sems)
    qring.start()

    def a_copy(o):
        peer = rem(head + o, 8)
        return pltpu.make_async_remote_copy(
            src_ref=wo_own.at[:, peer], dst_ref=wo_mid.at[head],
            send_sem=a_send.at[o], recv_sem=a_recv.at[head],
            device_id=(me, peer), device_id_type=MESH,
        )

    def a_arrival(o):
        peer = rem(head + o, 8)
        return pltpu.make_async_remote_copy(
            src_ref=wo_own.at[:, peer], dst_ref=wo_mid.at[peer],
            send_sem=a_send.at[o], recv_sem=a_recv.at[peer],
            device_id=(me, peer), device_id_type=MESH,
        )

    a_local = pltpu.make_async_copy(wo_own.at[:, head], wo_mid.at[head], local_sem.at[6])

    loop(8, lambda o: a_copy(o).start())
    a_local.start()

    for k in range(3):
        tell(token_sem.at[2 * k], up_dev)
        tell(token_sem.at[2 * k + 1], down_dev)
        pl.semaphore_wait(token_sem.at[2 * k], 1)
        pl.semaphore_wait(token_sem.at[2 * k + 1], 1)
    tell(token_sem.at[6], across_dev)
    pl.semaphore_wait(token_sem.at[6], 1)
    tell(token_sem.at[7], core_dev)
    pl.semaphore_wait(token_sem.at[7], 1)

    loads[4].wait()

    def add_squares(k, total):
        part = resid[:, pl.ds(pl.multiple_of(k * 512, 512), 512)].astype(jnp.float32)
        part = part * part
        return total + part[:, :128] + part[:, 128:256] + part[:, 256:384] + part[:, 384:]

    squares = lax.fori_loop(0, 16, add_squares, jnp.zeros((256, 128), jnp.float32))
    inv_ref[...] = lax.rsqrt(jnp.sum(squares, axis=1, keepdims=True) * (1.0 / 8192) + epsilon)

    loop(8, lambda o: a_arrival(o).wait_recv())
    a_local.wait()

    def b_copy(o):
        peer = rem(me + o, 32)
        return pltpu.make_async_remote_copy(
            src_ref=wo_mid.at[peer // 4, rem(peer, 4)], dst_ref=wo.at[head, me],
            send_sem=b_send.at[o], recv_sem=b_recv.at[me],
            device_id=(peer, head), device_id_type=MESH,
        )

    def b_arrival(o):
        peer = rem(me + o, 32)
        return pltpu.make_async_remote_copy(
            src_ref=wo_mid.at[peer // 4, rem(peer, 4)], dst_ref=wo.at[head, peer],
            send_sem=b_send.at[o], recv_sem=b_recv.at[peer],
            device_id=(peer, head), device_id_type=MESH,
        )

    b_local = pltpu.make_async_copy(
        wo_mid.at[me // 4, rem(me, 4)], wo.at[head, me], local_sem.at[7]
    )
    loop(32, lambda o: b_copy(o).start())
    b_local.start()

    acc[...] = jnp.zeros_like(acc)
    acc_kv[...] = jnp.zeros_like(acc_kv)
    acc_v[...] = jnp.zeros_like(acc_v)
    row = lax.broadcasted_iota(jnp.int32, (256, 256), 0)
    col = lax.broadcasted_iota(jnp.int32, (256, 256), 1)

    def column(values):
        return jnp.sum(jnp.where(row == col, values, 0.0), axis=1, keepdims=True)

    def project(chips, weights, total):
        for yy, zz in chips:
            at = pl.multiple_of((yy * 8 + zz) * 512, 512)
            part = resid[:, pl.ds(at, 512)].astype(jnp.float32)
            normed = (part * inv_ref[...] * gain_ref[:, pl.ds(at, 512)]).astype(jnp.bfloat16)
            total[...] += jnp.dot(
                normed, weights[yy, zz].reshape(512, -1), preferred_element_type=jnp.float32
            )

    def virtual_part(chips):
        for yy, zz in chips:
            for cc in range(2):
                j = seq_of(yy, zz, cc)
                gain = column(gain_ref[:, pl.ds(pl.multiple_of(j * 256, 256), 256)])
                scaled = (q_all[yy, zz, cc].astype(jnp.float32) * gain).astype(jnp.bfloat16)
                acc_v[...] += jnp.dot(
                    wo[:, j].reshape(128, 256), scaled, preferred_element_type=jnp.float32
                )

    def patch(chips):
        for yy, zz in chips:
            k = yy * 8 + zz
            rows = s_all[k // 2, :, pl.ds(pl.multiple_of(rem(k, 2) * 256, 256), 256)]
            acc[...] += inv_ref[...] * jnp.dot(
                rows, v_all[yy, zz].reshape(256, 512), preferred_element_type=jnp.float32
            )

    def take_q(chips):
        project(chips, q_all, acc)
        return chips

    def take_kv(chips):
        project(chips, kv_all, acc_kv)

    waiting = []
    qring.plane(1)
    loop(32, lambda o: b_arrival(o).wait_recv())
    b_local.wait()
    oring.start()
    waiting += take_q(qring.chips(0))
    oring.pair()
    qring.plane(2)
    waiting += take_q(qring.chips(1))
    oring.one(0)
    qring.other_start()
    qring.plane(3)
    oring.one(1)
    for k in (2, 3):
        loads[k].wait()
    kvring.start()
    loads[5].wait()
    sring.start()
    waiting += take_q(qring.chips(2))
    qring.other(1)
    qring.plane(4)
    waiting += take_q(qring.chips(3))
    qring.cross(0)
    qring.cross(1)
    qring.other(2)
    sring.pair()
    kvring.plane(1)
    waiting += take_q(qring.chips(4))
    oring.two(0)
    oring.two(1)
    virtual_part(waiting)
    qring.cross(2)
    qring.other(3)
    kvring.plane(2)
    for d in (0, 1, 2):
        virtual_part(take_q(qring.other_chips(d)))
    qring.cross(3)
    qring.other(4)
    qring.cross(4)
    kvring.other_start()
    sring.one(0)
    for d in (3, 4):
        virtual_part(take_q(qring.other_chips(d)))

    for r in range(4):
        cols = pl.ds(r * 128, 128)
        keep = edge_ref[me, head * 4 + r].astype(jnp.float32)
        v_all[y, z, c, :, cols] = (acc_v[:, cols] * keep).astype(jnp.bfloat16)
    vring.start()
    kvring.plane(3)
    sring.one(1)
    for d in (0, 1, 2):
        take_kv(kvring.chips(d))
    vring.plane(1)
    kvring.other(1)
    kvring.plane(4)
    vring.other_start()
    vring.plane(2)
    kvring.other(2)
    for d in (3, 4):
        take_kv(kvring.chips(d))
    sring.two(0)
    sring.two(1)
    patch(vring.chips(0))
    vring.other(1)
    vring.plane(3)
    kvring.other(3)
    patch(vring.chips(1))
    vring.other(2)
    vring.plane(4)
    for d in range(4):
        kvring.cross(d)
    kvring.other(4)
    kvring.cross(4)
    vring.cross(0)
    vring.cross(1)
    vring.other(3)
    patch(vring.chips(2))
    for d in range(5):
        take_kv(kvring.other_chips(d))
    patch(vring.other_chips(0))
    vring.cross(2)
    vring.other(4)
    patch(vring.chips(3))
    vring.cross(3)
    vring.cross(4)
    patch(vring.chips(4))
    keys = acc_kv[:, :128].astype(jnp.bfloat16)
    values = acc_kv[:, 128:].astype(jnp.bfloat16)
    for d in range(1, 5):
        patch(vring.other_chips(d))

    doc_row = doc_ref[...].astype(jnp.float32)
    allowed = (column(doc_row) == doc_row) & (col <= row)
    for r in range(4):
        cols = pl.ds(r * 128, 128)
        query = acc[:, cols].astype(jnp.bfloat16)
        scores = lax.dot_general(
            query, keys, (((1,), (1,)), ((), ())), preferred_element_type=jnp.float32
        ) * HEAD_SIZE ** (-0.5)
        scores = jnp.where(allowed, scores, -jnp.inf)
        weights = jnp.exp(scores - jnp.max(scores, axis=1, keepdims=True))
        weights = (weights / jnp.sum(weights, axis=1, keepdims=True)).astype(jnp.bfloat16)
        out_ref[:, cols] = jnp.dot(
            weights, values, preferred_element_type=jnp.float32
        ).astype(jnp.bfloat16)

    for ring in (qring, kvring, vring, oring, sring):
        ring.finish()
    loop(8, lambda o: a_copy(o).wait_send())
    loop(32, lambda o: b_copy(o).wait_send())


def local(resid, norm_gain, sender_diff, w_out1, w_query, w_key, w_value, edge_mask, doc_ids):
    dma = pltpu.SemaphoreType.DMA
    anywhere = pl.BlockSpec(memory_space=pl.ANY)
    vmem = pl.BlockSpec(memory_space=pltpu.VMEM)
    smem = pl.BlockSpec(memory_space=pltpu.SMEM)
    bf16, f32 = jnp.bfloat16, jnp.float32
    return pl.pallas_call(
        kernel,
        out_shape=jax.ShapeDtypeStruct((256, 512), bf16),
        in_specs=[
            anywhere, vmem, anywhere, anywhere, anywhere, anywhere, anywhere, smem, vmem,
        ],
        out_specs=vmem,
        scratch_shapes=[
            pltpu.VMEM((256, 8192), bf16),
            pltpu.VMEM((2, NZ, 2, 256, 512), bf16),
            pltpu.VMEM((2, NZ, 2, 256, 256), bf16),
            pltpu.VMEM((2, NZ, 2, 128, 512), bf16),
            pltpu.VMEM((8, 256, 512), bf16),
            pltpu.VMEM((8, 32, 16, 256), bf16),
            pltpu.VMEM((4, 8, 16, 256), bf16),
            pltpu.VMEM((8, 4, 16, 256), bf16),
            pltpu.VMEM((256, 512), f32),
            pltpu.VMEM((256, 256), f32),
            pltpu.VMEM((128, 512), f32),
            pltpu.VMEM((256, 1), f32),
            dma((8,)),
            pltpu.SemaphoreType.REGULAR((8,)),
            *[[dma((32,)), dma((32,)), dma((2,)), dma((52,))] for _ in range(3)],
            *[[dma((8,)), dma((2,)), dma((10,))] for _ in range(2)],
            dma((8,)), dma((8,)),
            dma((32,)), dma((32,)),
        ],
        compiler_params=pltpu.CompilerParams(
            collective_id=0, has_side_effects=True, vmem_limit_bytes=60 * 1024 * 1024
        ),
        name="patch_layer",
    )(
        resid,
        norm_gain.reshape(1, -1),
        sender_diff,
        w_out1.reshape(4, 8, 16, 256),
        w_query,
        w_key,
        w_value,
        edge_mask,
        doc_ids,
    )


def solution(mesh):
    placed = (
        P("seq", None),
        P(),
        P("seq", "head"),
        P("head", "seq"),
        P("seq", "head"),
        P("seq", "head"),
        P("seq", "head"),
        P(),
        P("seq", None),
    )
    return jax.shard_map(
        local, mesh=mesh, in_specs=placed, out_specs=P("seq", "head"), check_vma=False
    )
```

```python
import jax
import jax.numpy as jnp
from jax import lax
from jax.experimental import pallas as pl
from jax.experimental.pallas import tpu as pltpu
from jax.sharding import PartitionSpec as P

HEAD_SIZE = 128
epsilon = 1e-05
NZ = 8
MESH = pl.DeviceIdType.MESH


def rem(a, n):
    return lax.rem(a, n)


def kernel(
    resid_hbm, gain_ref, sender_hbm, out1_hbm, wq_hbm, wk_hbm, wv_hbm, edge_ref, doc_ref,
    out_ref,
    resid, qa_all, qb_all, kv_all, v_all, s_all, wo, wo_own, wo_mid, acc, acc_kv, acc_v, inv_ref,
    local_sem, token_sem, qa_sems, qb_sems, kv_sems, v_sems, wo_sems, s_sems,
    a_recv, a_send, b_recv, b_send,
):
    me = lax.axis_index("seq")
    head = lax.axis_index("head")
    y = me // 16
    z = rem(me // 2, NZ)
    c = rem(me, 2)
    oy, oc = 1 - y, 1 - c
    x = head // 2
    low = rem(head, 2)
    olow = 1 - low

    def seq_of(yy, zz, cc):
        return yy * 16 + zz * 2 + cc

    def at_z(step):
        return rem(z + (step + NZ), NZ)

    def at_x(step):
        return rem(x + (step + 4), 4)

    loads = [
        pltpu.make_async_copy(out1_hbm, wo_own, local_sem.at[0]),
        pltpu.make_async_copy(wq_hbm.at[:, pl.ds(0, 256)], qa_all.at[y, z, c], local_sem.at[1]),
        pltpu.make_async_copy(wk_hbm, kv_all.at[y, z, c, :, pl.ds(0, 128)], local_sem.at[2]),
        pltpu.make_async_copy(wv_hbm, kv_all.at[y, z, c, :, pl.ds(128, 128)], local_sem.at[3]),
        pltpu.make_async_copy(resid_hbm, resid, local_sem.at[4]),
        pltpu.make_async_copy(sender_hbm, s_all.at[head], local_sem.at[5]),
        pltpu.make_async_copy(wq_hbm.at[:, pl.ds(256, 256)], qb_all.at[y, z, c], local_sem.at[8]),
    ]
    for k in (1, 6, 0, 5, 4, 2, 3):
        loads[k].start()

    def loop(n, f):
        def body(o, _):
            f(o)
            return 0

        lax.fori_loop(1, n, body, 0)

    def tell(sem, device):
        pl.semaphore_signal(sem, inc=1, device_id=device, device_id_type=MESH)

    barrier = pltpu.get_barrier_semaphore()
    across_dev = (seq_of(oy, z, c), head)
    core_dev = (seq_of(y, z, oc), head)
    up_dev = (seq_of(y, at_z(1), c), head)
    down_dev = (seq_of(y, at_z(-1), c), head)
    for device in (across_dev, up_dev, down_dev, core_dev):
        tell(barrier, device)
    loop(8, lambda o: tell(barrier, (me, rem(head + o, 8))))
    for k in (1, 6, 0, 5):
        loads[k].wait()
    pl.semaphore_wait(barrier, 11)

    class Ring:
        def __init__(self, buf, sems, first):
            self.buf = buf
            self.recv, self.recv_b, self.half, self.send = sems
            self.rows = buf.shape[3]
            self.first = first
            self.whole = (0, self.rows)
            self.a = (0, first)
            self.b = (first, self.rows - first)
            self.sent = []

        def desc(self, slot, rows, device, recv, index=0):
            view = self.buf.at[slot[0], slot[1], slot[2], pl.ds(*rows)]
            return pltpu.make_async_remote_copy(
                src_ref=view, dst_ref=view, send_sem=self.send.at[index], recv_sem=recv,
                device_id=device, device_id_type=MESH,
            )

        def put(self, slot, rows, device, recv):
            copy = self.desc(slot, rows, device, recv, len(self.sent))
            copy.start()
            self.sent.append(copy)

        def got(self, slot, rows, recv):
            self.desc(slot, rows, core_dev, recv).wait_recv()

        def main(self, slot):
            return self.recv.at[seq_of(*slot)]

        def late(self, slot):
            return self.recv_b.at[seq_of(*slot)]

        def start(self):
            slot = (y, z, c)
            self.put(slot, self.whole, up_dev, self.main(slot))
            self.put(slot, self.whole, down_dev, self.main(slot))
            self.put(slot, self.a, across_dev, self.main(slot))
            self.put(slot, self.whole, core_dev, self.main(slot))
            self.put(slot, self.b, across_dev, self.late(slot))

        def round(self, yy, d, rows, kind):
            cut = (rows[0], rows[1] // 2), (rows[0] + rows[1] // 2, rows[1] // 2)
            if d == 4:
                slot = (yy, at_z(4), c)
                self.got(slot, cut[0], self.main(slot))
                self.got(slot, cut[1], self.half.at[kind])
                arrived = [slot]
            else:
                arrived = []
                for part, step, onward in ((0, 1, up_dev), (1, -1, down_dev)):
                    slot = (yy, at_z(-step * d), c)
                    self.got(slot, rows, self.main(slot))
                    if d < 3:
                        self.put(slot, rows, onward, self.main(slot))
                    else:
                        recv = self.half.at[kind] if part else self.main(slot)
                        self.put(slot, cut[part], onward, recv)
                    arrived.append(slot)
            for slot in arrived:
                if kind == 0:
                    self.put(slot, self.b, across_dev, self.late(slot))
                self.put(slot, rows, core_dev, self.main(slot))

        def plane(self, d):
            self.round(y, d, self.whole, 0)

        def other(self, d):
            self.round(oy, d, self.a, 1)

        def other_start(self):
            slot = (oy, z, c)
            self.got(slot, self.a, self.main(slot))
            self.put(slot, self.a, up_dev, self.main(slot))
            self.put(slot, self.a, down_dev, self.main(slot))
            self.put(slot, self.a, core_dev, self.main(slot))

        def places(self, d):
            return [at_z(d)] if d in (0, 4) else [at_z(-d), at_z(d)]

        def cross(self, d):
            for zz in self.places(d):
                slot = (oy, zz, c)
                self.got(slot, self.b, self.late(slot))
                self.put(slot, self.b, core_dev, self.late(slot))

        def chips(self, d):
            for zz in self.places(d):
                slot = (y, zz, oc)
                self.got(slot, self.whole, self.main(slot))
            return [(y, zz) for zz in self.places(d)]

        def other_chips(self, d):
            for zz in self.places(d):
                slot = (oy, zz, oc)
                self.got(slot, self.a, self.main(slot))
                self.got(slot, self.b, self.late(slot))
            return [(oy, zz) for zz in self.places(d)]

        def finish(self):
            for copy in self.sent:
                copy.wait_send()

    class HeadRing:
        def __init__(self, buf, sems):
            self.buf = buf
            self.recv, self.half, self.send = sems
            self.size = buf.shape[1]
            self.sent = []

        def desc(self, slot, rows, device, recv, index=0):
            view = self.buf.at[slot, pl.ds(*rows)]
            return pltpu.make_async_remote_copy(
                src_ref=view, dst_ref=view, send_sem=self.send.at[index], recv_sem=recv,
                device_id=device, device_id_type=MESH,
            )

        def put(self, slot, rows, step, recv, swap=False):
            device = (me, x * 2 + olow) if swap else (me, at_x(step) * 2 + low)
            copy = self.desc(slot, rows, device, recv, len(self.sent))
            copy.start()
            self.sent.append(copy)

        def got(self, slot, rows, recv):
            self.desc(slot, rows, (me, x * 2 + olow), recv).wait_recv()

        def start(self):
            whole = (0, self.size)
            for step in (1, -1):
                self.put(head, whole, step, self.recv.at[head])
            self.put(head, whole, 0, self.recv.at[head], swap=True)

        def pair(self):
            whole, slot = (0, self.size), x * 2 + olow
            self.got(slot, whole, self.recv.at[slot])
            for step in (1, -1):
                self.put(slot, whole, step, self.recv.at[slot])

        def one(self, kind):
            half = self.size // 2
            ll = olow if kind else low
            for part, step in ((0, 1), (1, -1)):
                slot = at_x(-step) * 2 + ll
                self.got(slot, (0, self.size), self.recv.at[slot])
                recv = self.half.at[kind] if part else self.recv.at[slot]
                self.put(slot, (part * half, half), step, recv)

        def two(self, kind):
            half = self.size // 2
            slot = at_x(2) * 2 + (olow if kind else low)
            self.got(slot, (0, half), self.recv.at[slot])
            self.got(slot, (half, half), self.half.at[kind])

        def finish(self):
            for copy in self.sent:
                copy.wait_send()

    qa_ring = Ring(qa_all, qa_sems, 128)
    qb_ring = Ring(qb_all, qb_sems, 128)
    kvring = Ring(kv_all, kv_sems, 128)
    vring = Ring(v_all, v_sems, 64)
    oring = HeadRing(wo, wo_sems)
    sring = HeadRing(s_all, s_sems)
    qa_ring.start()
    qb_ring.start()

    def a_copy(o):
        peer = rem(head + o, 8)
        return pltpu.make_async_remote_copy(
            src_ref=wo_own.at[:, peer], dst_ref=wo_mid.at[head],
            send_sem=a_send.at[o], recv_sem=a_recv.at[head],
            device_id=(me, peer), device_id_type=MESH,
        )

    def a_arrival(o):
        peer = rem(head + o, 8)
        return pltpu.make_async_remote_copy(
            src_ref=wo_own.at[:, peer], dst_ref=wo_mid.at[peer],
            send_sem=a_send.at[o], recv_sem=a_recv.at[peer],
            device_id=(me, peer), device_id_type=MESH,
        )

    a_local = pltpu.make_async_copy(wo_own.at[:, head], wo_mid.at[head], local_sem.at[6])

    loop(8, lambda o: a_copy(o).start())
    a_local.start()
    sring.start()

    for k in range(3):
        tell(token_sem.at[2 * k], up_dev)
        tell(token_sem.at[2 * k + 1], down_dev)
        pl.semaphore_wait(token_sem.at[2 * k], 1)
        pl.semaphore_wait(token_sem.at[2 * k + 1], 1)
    tell(token_sem.at[6], across_dev)
    pl.semaphore_wait(token_sem.at[6], 1)
    tell(token_sem.at[7], core_dev)
    pl.semaphore_wait(token_sem.at[7], 1)

    loads[4].wait()

    def add_squares(k, total):
        part = resid[:, pl.ds(pl.multiple_of(k * 512, 512), 512)].astype(jnp.float32)
        part = part * part
        return total + part[:, :128] + part[:, 128:256] + part[:, 256:384] + part[:, 384:]

    squares = lax.fori_loop(0, 16, add_squares, jnp.zeros((256, 128), jnp.float32))
    inv_ref[...] = lax.rsqrt(jnp.sum(squares, axis=1, keepdims=True) * (1.0 / 8192) + epsilon)

    loop(8, lambda o: a_arrival(o).wait_recv())
    a_local.wait()

    def b_copy(o):
        peer = rem(me + o, 32)
        return pltpu.make_async_remote_copy(
            src_ref=wo_mid.at[peer // 4, rem(peer, 4)], dst_ref=wo.at[head, me],
            send_sem=b_send.at[o], recv_sem=b_recv.at[me],
            device_id=(peer, head), device_id_type=MESH,
        )

    def b_arrival(o):
        peer = rem(me + o, 32)
        return pltpu.make_async_remote_copy(
            src_ref=wo_mid.at[peer // 4, rem(peer, 4)], dst_ref=wo.at[head, peer],
            send_sem=b_send.at[o], recv_sem=b_recv.at[peer],
            device_id=(peer, head), device_id_type=MESH,
        )

    b_local = pltpu.make_async_copy(
        wo_mid.at[me // 4, rem(me, 4)], wo.at[head, me], local_sem.at[7]
    )
    loop(32, lambda o: b_copy(o).start())
    b_local.start()

    acc[...] = jnp.zeros_like(acc)
    acc_kv[...] = jnp.zeros_like(acc_kv)
    acc_v[...] = jnp.zeros_like(acc_v)
    row = lax.broadcasted_iota(jnp.int32, (256, 256), 0)
    col = lax.broadcasted_iota(jnp.int32, (256, 256), 1)

    def column(values):
        return jnp.sum(jnp.where(row == col, values, 0.0), axis=1, keepdims=True)

    def project(chips, pairs):
        for yy, zz in chips:
            at = pl.multiple_of((yy * 8 + zz) * 512, 512)
            part = resid[:, pl.ds(at, 512)].astype(jnp.float32)
            normed = (part * inv_ref[...] * gain_ref[:, pl.ds(at, 512)]).astype(jnp.bfloat16)
            for weights, total, cols in pairs:
                total[:, cols] += jnp.dot(
                    normed, weights[yy, zz].reshape(512, 256), preferred_element_type=jnp.float32
                )

    left, right = pl.ds(0, 256), pl.ds(256, 256)

    def virtual_part(chips):
        for yy, zz in chips:
            for cc in range(2):
                j = seq_of(yy, zz, cc)
                gain = column(gain_ref[:, pl.ds(pl.multiple_of(j * 256, 256), 256)])
                for weights, cols in ((qa_all, left), (qb_all, right)):
                    scaled = (weights[yy, zz, cc].astype(jnp.float32) * gain).astype(jnp.bfloat16)
                    acc_v[:, cols] += jnp.dot(
                        wo[:, j].reshape(128, 256), scaled, preferred_element_type=jnp.float32
                    )

    def patch(chips):
        for yy, zz in chips:
            k = yy * 8 + zz
            rows = s_all[k // 2, :, pl.ds(pl.multiple_of(rem(k, 2) * 256, 256), 256)]
            acc[...] += inv_ref[...] * jnp.dot(
                rows, v_all[yy, zz].reshape(256, 512), preferred_element_type=jnp.float32
            )

    class Both:
        def __getattr__(self, name):
            def call(*args):
                getattr(qa_ring, name)(*args)
                return getattr(qb_ring, name)(*args)

            return call

    qring = Both()

    def take_q(chips):
        project(chips, ((qa_all, acc, left), (qb_all, acc, right)))
        return chips

    def take_kv(chips):
        project(chips, ((kv_all, acc_kv, left),))

    waiting = []
    qring.plane(1)
    loop(32, lambda o: b_arrival(o).wait_recv())
    b_local.wait()
    oring.start()
    waiting += take_q(qring.chips(0))
    qring.plane(2)
    qring.other_start()
    waiting += take_q(qring.chips(1))
    sring.pair()
    oring.one(0)
    qring.plane(3)
    for k in (2, 3):
        loads[k].wait()
    kvring.start()
    oring.pair()
    qring.other(1)
    sring.one(0)
    waiting += take_q(qring.chips(2))
    qring.plane(4)
    kvring.plane(1)
    qring.other(2)
    waiting += take_q(qring.chips(3))
    oring.one(1)
    sring.one(1)
    kvring.plane(2)
    qring.cross(0)
    qring.cross(1)
    qring.other(3)
    waiting += take_q(qring.chips(4))
    oring.two(0)
    kvring.other_start()
    oring.two(1)
    virtual_part(waiting)
    kvring.plane(3)
    qring.cross(2)
    qring.other(4)
    for d in (0, 1, 2):
        virtual_part(take_q(qring.other_chips(d)))
    qring.cross(3)
    qring.cross(4)
    for d in (3, 4):
        virtual_part(take_q(qring.other_chips(d)))

    for r in range(4):
        cols = pl.ds(r * 128, 128)
        keep = edge_ref[me, head * 4 + r].astype(jnp.float32)
        v_all[y, z, c, :, cols] = (acc_v[:, cols] * keep).astype(jnp.bfloat16)
    vring.start()
    kvring.other(1)
    for d in (0, 1, 2):
        take_kv(kvring.chips(d))
    vring.plane(1)
    kvring.plane(4)
    vring.other_start()
    kvring.other(2)
    vring.plane(2)
    for d in (3, 4):
        take_kv(kvring.chips(d))
    sring.two(0)
    sring.two(1)
    patch(vring.chips(0))
    kvring.other(3)
    vring.other(1)
    vring.plane(3)
    patch(vring.chips(1))
    kvring.other(4)
    vring.other(2)
    vring.plane(4)
    for d in range(5):
        kvring.cross(d)
    vring.cross(0)
    vring.cross(1)
    vring.other(3)
    patch(vring.chips(2))
    for d in range(5):
        take_kv(kvring.other_chips(d))
    patch(vring.other_chips(0))
    vring.cross(2)
    vring.other(4)
    patch(vring.chips(3))
    vring.cross(3)
    vring.cross(4)
    patch(vring.chips(4))
    keys = acc_kv[:, :128].astype(jnp.bfloat16)
    values = acc_kv[:, 128:].astype(jnp.bfloat16)
    for d in range(1, 5):
        patch(vring.other_chips(d))

    doc_row = doc_ref[...].astype(jnp.float32)
    allowed = (column(doc_row) == doc_row) & (col <= row)
    for r in range(4):
        cols = pl.ds(r * 128, 128)
        query = acc[:, cols].astype(jnp.bfloat16)
        scores = lax.dot_general(
            query, keys, (((1,), (1,)), ((), ())), preferred_element_type=jnp.float32
        ) * HEAD_SIZE ** (-0.5)
        scores = jnp.where(allowed, scores, -jnp.inf)
        weights = jnp.exp(scores - jnp.max(scores, axis=1, keepdims=True))
        weights = (weights / jnp.sum(weights, axis=1, keepdims=True)).astype(jnp.bfloat16)
        out_ref[:, cols] = jnp.dot(
            weights, values, preferred_element_type=jnp.float32
        ).astype(jnp.bfloat16)

    for ring in (qa_ring, qb_ring, kvring, vring, oring, sring):
        ring.finish()
    loop(8, lambda o: a_copy(o).wait_send())
    loop(32, lambda o: b_copy(o).wait_send())


def local(resid, norm_gain, sender_diff, w_out1, w_query, w_key, w_value, edge_mask, doc_ids):
    dma = pltpu.SemaphoreType.DMA
    anywhere = pl.BlockSpec(memory_space=pl.ANY)
    vmem = pl.BlockSpec(memory_space=pltpu.VMEM)
    smem = pl.BlockSpec(memory_space=pltpu.SMEM)
    bf16, f32 = jnp.bfloat16, jnp.float32
    return pl.pallas_call(
        kernel,
        out_shape=jax.ShapeDtypeStruct((256, 512), bf16),
        in_specs=[
            anywhere, vmem, anywhere, anywhere, anywhere, anywhere, anywhere, smem, vmem,
        ],
        out_specs=vmem,
        scratch_shapes=[
            pltpu.VMEM((256, 8192), bf16),
            pltpu.VMEM((2, NZ, 2, 256, 256), bf16),
            pltpu.VMEM((2, NZ, 2, 256, 256), bf16),
            pltpu.VMEM((2, NZ, 2, 256, 256), bf16),
            pltpu.VMEM((2, NZ, 2, 128, 512), bf16),
            pltpu.VMEM((8, 256, 512), bf16),
            pltpu.VMEM((8, 32, 16, 256), bf16),
            pltpu.VMEM((4, 8, 16, 256), bf16),
            pltpu.VMEM((8, 4, 16, 256), bf16),
            pltpu.VMEM((256, 512), f32),
            pltpu.VMEM((256, 256), f32),
            pltpu.VMEM((128, 512), f32),
            pltpu.VMEM((256, 1), f32),
            dma((9,)),
            pltpu.SemaphoreType.REGULAR((8,)),
            *[[dma((32,)), dma((32,)), dma((2,)), dma((52,))] for _ in range(4)],
            *[[dma((8,)), dma((2,)), dma((10,))] for _ in range(2)],
            dma((8,)), dma((8,)),
            dma((32,)), dma((32,)),
        ],
        compiler_params=pltpu.CompilerParams(
            collective_id=0, has_side_effects=True, vmem_limit_bytes=60 * 1024 * 1024
        ),
        name="patch_layer",
    )(
        resid,
        norm_gain.reshape(1, -1),
        sender_diff,
        w_out1.reshape(4, 8, 16, 256),
        w_query,
        w_key,
        w_value,
        edge_mask,
        doc_ids,
    )


def solution(mesh):
    placed = (
        P("seq", None),
        P(),
        P("seq", "head"),
        P("head", "seq"),
        P("seq", "head"),
        P("seq", "head"),
        P("seq", "head"),
        P(),
        P("seq", None),
    )
    return jax.shard_map(
        local, mesh=mesh, in_specs=placed, out_specs=P("seq", "head"), check_vma=False
    )
```

```python
import jax
import jax.numpy as jnp
from jax import lax
from jax.experimental import pallas as pl
from jax.experimental.pallas import tpu as pltpu
from jax.sharding import PartitionSpec as P

HEAD_SIZE = 128
epsilon = 1e-05
NZ = 8
MESH = pl.DeviceIdType.MESH


def rem(a, n):
    return lax.rem(a, n)


def kernel(
    resid_hbm, gain_ref, sender_hbm, out1_hbm, wq_hbm, wk_hbm, wv_hbm, edge_ref, doc_ref,
    out_ref,
    resid, qa_all, qb_all, kv_all, v_all, s_all, wo, wo_own, wo_mid, acc, acc_kv, acc_v, inv_ref,
    local_sem, token_sem, qa_sems, qb_sems, kv_sems, v_sems, wo_sems, s_sems,
    a_recv, a_send, b_recv, b_send,
):
    me = lax.axis_index("seq")
    head = lax.axis_index("head")
    y = me // 16
    z = rem(me // 2, NZ)
    c = rem(me, 2)
    oy, oc = 1 - y, 1 - c
    x = head // 2
    low = rem(head, 2)
    olow = 1 - low

    def seq_of(yy, zz, cc):
        return yy * 16 + zz * 2 + cc

    def at_z(step):
        return rem(z + (step + NZ), NZ)

    def at_x(step):
        return rem(x + (step + 4), 4)

    loads = [
        pltpu.make_async_copy(out1_hbm, wo_own, local_sem.at[0]),
        pltpu.make_async_copy(wq_hbm.at[:, pl.ds(0, 256)], qa_all.at[y, z, c], local_sem.at[1]),
        pltpu.make_async_copy(wk_hbm, kv_all.at[y, z, c, :, pl.ds(0, 128)], local_sem.at[2]),
        pltpu.make_async_copy(wv_hbm, kv_all.at[y, z, c, :, pl.ds(128, 128)], local_sem.at[3]),
        pltpu.make_async_copy(resid_hbm, resid, local_sem.at[4]),
        pltpu.make_async_copy(sender_hbm, s_all.at[head], local_sem.at[5]),
        pltpu.make_async_copy(wq_hbm.at[:, pl.ds(256, 256)], qb_all.at[y, z, c], local_sem.at[8]),
    ]
    for k in (1, 6, 0, 5, 4, 2, 3):
        loads[k].start()

    def loop(n, f):
        def body(o, _):
            f(o)
            return 0

        lax.fori_loop(1, n, body, 0)

    def tell(sem, device):
        pl.semaphore_signal(sem, inc=1, device_id=device, device_id_type=MESH)

    barrier = pltpu.get_barrier_semaphore()
    across_dev = (seq_of(oy, z, c), head)
    core_dev = (seq_of(y, z, oc), head)
    up_dev = (seq_of(y, at_z(1), c), head)
    down_dev = (seq_of(y, at_z(-1), c), head)
    for device in (across_dev, up_dev, down_dev, core_dev):
        tell(barrier, device)
    loop(8, lambda o: tell(barrier, (me, rem(head + o, 8))))
    for k in (1, 6, 0, 5):
        loads[k].wait()
    pl.semaphore_wait(barrier, 11)

    class Ring:
        def __init__(self, buf, sems, first):
            self.buf = buf
            self.recv, self.recv_b, self.half, self.send = sems
            self.rows = buf.shape[3]
            self.first = first
            self.whole = (0, self.rows)
            self.a = (0, first)
            self.b = (first, self.rows - first)
            self.sent = []

        def desc(self, slot, rows, device, recv, index=0):
            view = self.buf.at[slot[0], slot[1], slot[2], pl.ds(*rows)]
            return pltpu.make_async_remote_copy(
                src_ref=view, dst_ref=view, send_sem=self.send.at[index], recv_sem=recv,
                device_id=device, device_id_type=MESH,
            )

        def put(self, slot, rows, device, recv):
            copy = self.desc(slot, rows, device, recv, len(self.sent))
            copy.start()
            self.sent.append(copy)

        def got(self, slot, rows, recv):
            self.desc(slot, rows, core_dev, recv).wait_recv()

        def main(self, slot):
            return self.recv.at[seq_of(*slot)]

        def late(self, slot):
            return self.recv_b.at[seq_of(*slot)]

        def start(self):
            slot = (y, z, c)
            self.put(slot, self.whole, up_dev, self.main(slot))
            self.put(slot, self.whole, down_dev, self.main(slot))
            self.put(slot, self.a, across_dev, self.main(slot))
            self.put(slot, self.whole, core_dev, self.main(slot))

        def own_across(self):
            slot = (y, z, c)
            self.put(slot, self.b, across_dev, self.late(slot))

        def round(self, yy, d, rows, kind):
            cut = (rows[0], rows[1] // 2), (rows[0] + rows[1] // 2, rows[1] // 2)
            if d == 4:
                slot = (yy, at_z(4), c)
                self.got(slot, cut[0], self.main(slot))
                self.got(slot, cut[1], self.half.at[kind])
                arrived = [slot]
            else:
                arrived = []
                for part, step, onward in ((0, 1, up_dev), (1, -1, down_dev)):
                    slot = (yy, at_z(-step * d), c)
                    self.got(slot, rows, self.main(slot))
                    if d < 3:
                        self.put(slot, rows, onward, self.main(slot))
                    else:
                        recv = self.half.at[kind] if part else self.main(slot)
                        self.put(slot, cut[part], onward, recv)
                    arrived.append(slot)
            for slot in arrived:
                if kind == 0:
                    self.put(slot, self.b, across_dev, self.late(slot))
                self.put(slot, rows, core_dev, self.main(slot))

        def plane(self, d):
            self.round(y, d, self.whole, 0)

        def other(self, d):
            self.round(oy, d, self.a, 1)

        def other_start(self):
            slot = (oy, z, c)
            self.got(slot, self.a, self.main(slot))
            self.put(slot, self.a, up_dev, self.main(slot))
            self.put(slot, self.a, down_dev, self.main(slot))
            self.put(slot, self.a, core_dev, self.main(slot))

        def places(self, d):
            return [at_z(d)] if d in (0, 4) else [at_z(-d), at_z(d)]

        def cross(self, d):
            for zz in self.places(d):
                slot = (oy, zz, c)
                self.got(slot, self.b, self.late(slot))
                self.put(slot, self.b, core_dev, self.late(slot))

        def chips(self, d):
            for zz in self.places(d):
                slot = (y, zz, oc)
                self.got(slot, self.whole, self.main(slot))
            return [(y, zz) for zz in self.places(d)]

        def other_chips(self, d):
            for zz in self.places(d):
                slot = (oy, zz, oc)
                self.got(slot, self.a, self.main(slot))
                self.got(slot, self.b, self.late(slot))
            return [(oy, zz) for zz in self.places(d)]

        def finish(self):
            for copy in self.sent:
                copy.wait_send()

    class HeadRing:
        def __init__(self, buf, sems):
            self.buf = buf
            self.recv, self.half, self.send = sems
            self.size = buf.shape[1]
            self.sent = []

        def desc(self, slot, rows, device, recv, index=0):
            view = self.buf.at[slot, pl.ds(*rows)]
            return pltpu.make_async_remote_copy(
                src_ref=view, dst_ref=view, send_sem=self.send.at[index], recv_sem=recv,
                device_id=device, device_id_type=MESH,
            )

        def put(self, slot, rows, step, recv, swap=False):
            device = (me, x * 2 + olow) if swap else (me, at_x(step) * 2 + low)
            copy = self.desc(slot, rows, device, recv, len(self.sent))
            copy.start()
            self.sent.append(copy)

        def got(self, slot, rows, recv):
            self.desc(slot, rows, (me, x * 2 + olow), recv).wait_recv()

        def start(self):
            whole = (0, self.size)
            for step in (1, -1):
                self.put(head, whole, step, self.recv.at[head])
            self.put(head, whole, 0, self.recv.at[head], swap=True)

        def pair(self):
            whole, slot = (0, self.size), x * 2 + olow
            self.got(slot, whole, self.recv.at[slot])
            for step in (1, -1):
                self.put(slot, whole, step, self.recv.at[slot])

        def one(self, kind):
            half = self.size // 2
            ll = olow if kind else low
            for part, step in ((0, 1), (1, -1)):
                slot = at_x(-step) * 2 + ll
                self.got(slot, (0, self.size), self.recv.at[slot])
                recv = self.half.at[kind] if part else self.recv.at[slot]
                self.put(slot, (part * half, half), step, recv)

        def two(self, kind):
            half = self.size // 2
            slot = at_x(2) * 2 + (olow if kind else low)
            self.got(slot, (0, half), self.recv.at[slot])
            self.got(slot, (half, half), self.half.at[kind])

        def finish(self):
            for copy in self.sent:
                copy.wait_send()

    qa_ring = Ring(qa_all, qa_sems, 128)
    qb_ring = Ring(qb_all, qb_sems, 128)
    kvring = Ring(kv_all, kv_sems, 128)
    vring = Ring(v_all, v_sems, 64)
    oring = HeadRing(wo, wo_sems)
    sring = HeadRing(s_all, s_sems)
    def a_copy(o):
        peer = rem(head + o, 8)
        return pltpu.make_async_remote_copy(
            src_ref=wo_own.at[:, peer], dst_ref=wo_mid.at[head],
            send_sem=a_send.at[o], recv_sem=a_recv.at[head],
            device_id=(me, peer), device_id_type=MESH,
        )

    def a_arrival(o):
        peer = rem(head + o, 8)
        return pltpu.make_async_remote_copy(
            src_ref=wo_own.at[:, peer], dst_ref=wo_mid.at[peer],
            send_sem=a_send.at[o], recv_sem=a_recv.at[peer],
            device_id=(me, peer), device_id_type=MESH,
        )

    a_local = pltpu.make_async_copy(wo_own.at[:, head], wo_mid.at[head], local_sem.at[6])

    loop(8, lambda o: a_copy(o).start())
    a_local.start()
    qa_ring.start()
    qb_ring.start()
    sring.start()

    for k in range(3):
        tell(token_sem.at[2 * k], up_dev)
        tell(token_sem.at[2 * k + 1], down_dev)
        pl.semaphore_wait(token_sem.at[2 * k], 1)
        pl.semaphore_wait(token_sem.at[2 * k + 1], 1)
    tell(token_sem.at[6], across_dev)
    pl.semaphore_wait(token_sem.at[6], 1)
    tell(token_sem.at[7], core_dev)
    pl.semaphore_wait(token_sem.at[7], 1)

    loop(8, lambda o: a_arrival(o).wait_recv())
    a_local.wait()

    def b_copy(o):
        peer = rem(me + o, 32)
        return pltpu.make_async_remote_copy(
            src_ref=wo_mid.at[peer // 4, rem(peer, 4)], dst_ref=wo.at[head, me],
            send_sem=b_send.at[o], recv_sem=b_recv.at[me],
            device_id=(peer, head), device_id_type=MESH,
        )

    def b_arrival(o):
        peer = rem(me + o, 32)
        return pltpu.make_async_remote_copy(
            src_ref=wo_mid.at[peer // 4, rem(peer, 4)], dst_ref=wo.at[head, peer],
            send_sem=b_send.at[o], recv_sem=b_recv.at[peer],
            device_id=(peer, head), device_id_type=MESH,
        )

    b_local = pltpu.make_async_copy(
        wo_mid.at[me // 4, rem(me, 4)], wo.at[head, me], local_sem.at[7]
    )
    loop(32, lambda o: b_copy(o).start())
    b_local.start()

    loads[4].wait()

    def add_squares(k, total):
        part = resid[:, pl.ds(pl.multiple_of(k * 512, 512), 512)].astype(jnp.float32)
        part = part * part
        return total + part[:, :128] + part[:, 128:256] + part[:, 256:384] + part[:, 384:]

    squares = lax.fori_loop(0, 16, add_squares, jnp.zeros((256, 128), jnp.float32))
    inv_ref[...] = lax.rsqrt(jnp.sum(squares, axis=1, keepdims=True) * (1.0 / 8192) + epsilon)

    acc[...] = jnp.zeros_like(acc)
    acc_kv[...] = jnp.zeros_like(acc_kv)
    acc_v[...] = jnp.zeros_like(acc_v)
    row = lax.broadcasted_iota(jnp.int32, (256, 256), 0)
    col = lax.broadcasted_iota(jnp.int32, (256, 256), 1)

    def column(values):
        return jnp.sum(jnp.where(row == col, values, 0.0), axis=1, keepdims=True)

    def project(chips, pairs):
        for yy, zz in chips:
            at = pl.multiple_of((yy * 8 + zz) * 512, 512)
            part = resid[:, pl.ds(at, 512)].astype(jnp.float32)
            normed = (part * inv_ref[...] * gain_ref[:, pl.ds(at, 512)]).astype(jnp.bfloat16)
            for weights, total, cols in pairs:
                total[:, cols] += jnp.dot(
                    normed, weights[yy, zz].reshape(512, 256), preferred_element_type=jnp.float32
                )

    left, right = pl.ds(0, 256), pl.ds(256, 256)

    def virtual_part(chips):
        for yy, zz in chips:
            for cc in range(2):
                j = seq_of(yy, zz, cc)
                gain = column(gain_ref[:, pl.ds(pl.multiple_of(j * 256, 256), 256)])
                for weights, cols in ((qa_all, left), (qb_all, right)):
                    scaled = (weights[yy, zz, cc].astype(jnp.float32) * gain).astype(jnp.bfloat16)
                    acc_v[:, cols] += jnp.dot(
                        wo[:, j].reshape(128, 256), scaled, preferred_element_type=jnp.float32
                    )

    def patch(chips):
        for yy, zz in chips:
            k = yy * 8 + zz
            rows = s_all[k // 2, :, pl.ds(pl.multiple_of(rem(k, 2) * 256, 256), 256)]
            acc[...] += inv_ref[...] * jnp.dot(
                rows, v_all[yy, zz].reshape(256, 512), preferred_element_type=jnp.float32
            )

    class Both:
        def __getattr__(self, name):
            def call(*args):
                getattr(qa_ring, name)(*args)
                return getattr(qb_ring, name)(*args)

            return call

    qring = Both()

    def take_q(chips):
        project(chips, ((qa_all, acc, left), (qb_all, acc, right)))
        return chips

    def take_kv(chips):
        project(chips, ((kv_all, acc_kv, left),))

    waiting = []
    qring.plane(1)
    loop(32, lambda o: b_arrival(o).wait_recv())
    b_local.wait()
    oring.start()
    qring.own_across()
    waiting += take_q(qring.chips(0))
    qring.plane(2)
    qring.other_start()
    waiting += take_q(qring.chips(1))
    sring.pair()
    oring.one(0)
    qring.plane(3)
    for k in (2, 3):
        loads[k].wait()
    kvring.start()
    kvring.own_across()
    oring.pair()
    qring.other(1)
    sring.one(0)
    waiting += take_q(qring.chips(2))
    qring.plane(4)
    kvring.plane(1)
    qring.other(2)
    waiting += take_q(qring.chips(3))
    oring.one(1)
    sring.one(1)
    kvring.plane(2)
    qring.cross(0)
    qring.cross(1)
    qring.other(3)
    waiting += take_q(qring.chips(4))
    oring.two(0)
    kvring.other_start()
    oring.two(1)
    virtual_part(waiting)
    kvring.plane(3)
    qring.cross(2)
    qring.other(4)
    for d in (0, 1, 2):
        virtual_part(take_q(qring.other_chips(d)))
    qring.cross(3)
    qring.cross(4)
    for d in (3, 4):
        virtual_part(take_q(qring.other_chips(d)))

    for r in range(4):
        cols = pl.ds(r * 128, 128)
        keep = edge_ref[me, head * 4 + r].astype(jnp.float32)
        v_all[y, z, c, :, cols] = (acc_v[:, cols] * keep).astype(jnp.bfloat16)
    vring.start()
    vring.own_across()
    kvring.other(1)
    for d in (0, 1, 2):
        take_kv(kvring.chips(d))
    vring.plane(1)
    kvring.plane(4)
    vring.other_start()
    kvring.other(2)
    vring.plane(2)
    for d in (3, 4):
        take_kv(kvring.chips(d))
    sring.two(0)
    sring.two(1)
    patch(vring.chips(0))
    kvring.other(3)
    vring.other(1)
    vring.plane(3)
    patch(vring.chips(1))
    kvring.other(4)
    vring.other(2)
    vring.plane(4)
    for d in range(5):
        kvring.cross(d)
    vring.cross(0)
    vring.cross(1)
    vring.other(3)
    patch(vring.chips(2))
    for d in range(5):
        take_kv(kvring.other_chips(d))
    patch(vring.other_chips(0))
    vring.cross(2)
    vring.other(4)
    patch(vring.chips(3))
    vring.cross(3)
    vring.cross(4)
    patch(vring.chips(4))
    keys = acc_kv[:, :128].astype(jnp.bfloat16)
    values = acc_kv[:, 128:].astype(jnp.bfloat16)
    for d in range(1, 5):
        patch(vring.other_chips(d))

    doc_row = doc_ref[...].astype(jnp.float32)
    allowed = (column(doc_row) == doc_row) & (col <= row)
    for r in range(4):
        cols = pl.ds(r * 128, 128)
        query = acc[:, cols].astype(jnp.bfloat16)
        scores = lax.dot_general(
            query, keys, (((1,), (1,)), ((), ())), preferred_element_type=jnp.float32
        ) * HEAD_SIZE ** (-0.5)
        scores = jnp.where(allowed, scores, -jnp.inf)
        weights = jnp.exp(scores - jnp.max(scores, axis=1, keepdims=True))
        weights = (weights / jnp.sum(weights, axis=1, keepdims=True)).astype(jnp.bfloat16)
        out_ref[:, cols] = jnp.dot(
            weights, values, preferred_element_type=jnp.float32
        ).astype(jnp.bfloat16)

    for ring in (qa_ring, qb_ring, kvring, vring, oring, sring):
        ring.finish()
    loop(8, lambda o: a_copy(o).wait_send())
    loop(32, lambda o: b_copy(o).wait_send())


def local(resid, norm_gain, sender_diff, w_out1, w_query, w_key, w_value, edge_mask, doc_ids):
    dma = pltpu.SemaphoreType.DMA
    anywhere = pl.BlockSpec(memory_space=pl.ANY)
    vmem = pl.BlockSpec(memory_space=pltpu.VMEM)
    smem = pl.BlockSpec(memory_space=pltpu.SMEM)
    bf16, f32 = jnp.bfloat16, jnp.float32
    return pl.pallas_call(
        kernel,
        out_shape=jax.ShapeDtypeStruct((256, 512), bf16),
        in_specs=[
            anywhere, vmem, anywhere, anywhere, anywhere, anywhere, anywhere, smem, vmem,
        ],
        out_specs=vmem,
        scratch_shapes=[
            pltpu.VMEM((256, 8192), bf16),
            pltpu.VMEM((2, NZ, 2, 256, 256), bf16),
            pltpu.VMEM((2, NZ, 2, 256, 256), bf16),
            pltpu.VMEM((2, NZ, 2, 256, 256), bf16),
            pltpu.VMEM((2, NZ, 2, 128, 512), bf16),
            pltpu.VMEM((8, 256, 512), bf16),
            pltpu.VMEM((8, 32, 16, 256), bf16),
            pltpu.VMEM((4, 8, 16, 256), bf16),
            pltpu.VMEM((8, 4, 16, 256), bf16),
            pltpu.VMEM((256, 512), f32),
            pltpu.VMEM((256, 256), f32),
            pltpu.VMEM((128, 512), f32),
            pltpu.VMEM((256, 1), f32),
            dma((9,)),
            pltpu.SemaphoreType.REGULAR((8,)),
            *[[dma((32,)), dma((32,)), dma((2,)), dma((52,))] for _ in range(4)],
            *[[dma((8,)), dma((2,)), dma((10,))] for _ in range(2)],
            dma((8,)), dma((8,)),
            dma((32,)), dma((32,)),
        ],
        compiler_params=pltpu.CompilerParams(
            collective_id=0, has_side_effects=True, vmem_limit_bytes=60 * 1024 * 1024
        ),
        name="patch_layer",
    )(
        resid,
        norm_gain.reshape(1, -1),
        sender_diff,
        w_out1.reshape(4, 8, 16, 256),
        w_query,
        w_key,
        w_value,
        edge_mask,
        doc_ids,
    )


def solution(mesh):
    placed = (
        P("seq", None),
        P(),
        P("seq", "head"),
        P("head", "seq"),
        P("seq", "head"),
        P("seq", "head"),
        P("seq", "head"),
        P(),
        P("seq", None),
    )
    return jax.shard_map(
        local, mesh=mesh, in_specs=placed, out_specs=P("seq", "head"), check_vma=False
    )
```

```python
import jax
import jax.numpy as jnp
from jax import lax
from jax.experimental import pallas as pl
from jax.experimental.pallas import tpu as pltpu
from jax.sharding import PartitionSpec as P

HEAD_SIZE = 128
epsilon = 1e-05
NZ = 8
MESH = pl.DeviceIdType.MESH


def rem(a, n):
    return lax.rem(a, n)


def kernel(
    resid_hbm, gain_ref, sender_hbm, out1_hbm, wq_hbm, wk_hbm, wv_hbm, edge_ref, doc_ref,
    out_ref,
    resid, qa_all, qb_all, kv_all, v_all, s_all, wo, wo_own, wo_mid, acc, acc_kv, acc_v, inv_ref,
    local_sem, token_sem, qa_sems, qb_sems, kv_sems, v_sems, wo_sems, s_sems,
    a_recv, a_send, b_recv, b_send,
):
    me = lax.axis_index("seq")
    head = lax.axis_index("head")
    y = me // 16
    z = rem(me // 2, NZ)
    c = rem(me, 2)
    oy, oc = 1 - y, 1 - c
    x = head // 2
    low = rem(head, 2)
    olow = 1 - low

    def seq_of(yy, zz, cc):
        return yy * 16 + zz * 2 + cc

    def at_z(step):
        return rem(z + (step + NZ), NZ)

    def at_x(step):
        return rem(x + (step + 4), 4)

    loads = [
        pltpu.make_async_copy(out1_hbm, wo_own, local_sem.at[0]),
        pltpu.make_async_copy(wq_hbm.at[:, pl.ds(0, 256)], qa_all.at[y, z, c], local_sem.at[1]),
        pltpu.make_async_copy(wk_hbm, kv_all.at[y, z, c, :, pl.ds(0, 128)], local_sem.at[2]),
        pltpu.make_async_copy(wv_hbm, kv_all.at[y, z, c, :, pl.ds(128, 128)], local_sem.at[3]),
        pltpu.make_async_copy(resid_hbm, resid, local_sem.at[4]),
        pltpu.make_async_copy(sender_hbm, s_all.at[head], local_sem.at[5]),
        pltpu.make_async_copy(wq_hbm.at[:, pl.ds(256, 256)], qb_all.at[y, z, c], local_sem.at[8]),
    ]
    for k in (1, 6, 0, 5, 4, 2, 3):
        loads[k].start()

    def loop(n, f):
        def body(o, _):
            f(o)
            return 0

        lax.fori_loop(1, n, body, 0)

    def tell(sem, device):
        pl.semaphore_signal(sem, inc=1, device_id=device, device_id_type=MESH)

    barrier = pltpu.get_barrier_semaphore()
    across_dev = (seq_of(oy, z, c), head)
    core_dev = (seq_of(y, z, oc), head)
    up_dev = (seq_of(y, at_z(1), c), head)
    down_dev = (seq_of(y, at_z(-1), c), head)
    for device in (across_dev, up_dev, down_dev, core_dev):
        tell(barrier, device)
    loop(8, lambda o: tell(barrier, (me, rem(head + o, 8))))
    for k in (1, 6, 0, 5):
        loads[k].wait()
    pl.semaphore_wait(barrier, 11)

    class Ring:
        def __init__(self, buf, sems, first):
            self.buf = buf
            self.recv, self.recv_b, self.half, self.send = sems
            self.rows = buf.shape[3]
            self.first = first
            self.whole = (0, self.rows)
            self.a = (0, first)
            self.b = (first, self.rows - first)
            self.sent = []

        def desc(self, slot, rows, device, recv, index=0):
            view = self.buf.at[slot[0], slot[1], slot[2], pl.ds(*rows)]
            return pltpu.make_async_remote_copy(
                src_ref=view, dst_ref=view, send_sem=self.send.at[index], recv_sem=recv,
                device_id=device, device_id_type=MESH,
            )

        def put(self, slot, rows, device, recv):
            copy = self.desc(slot, rows, device, recv, len(self.sent))
            copy.start()
            self.sent.append(copy)

        def got(self, slot, rows, recv):
            self.desc(slot, rows, core_dev, recv).wait_recv()

        def main(self, slot):
            return self.recv.at[seq_of(*slot)]

        def late(self, slot):
            return self.recv_b.at[seq_of(*slot)]

        def start(self):
            slot = (y, z, c)
            self.put(slot, self.whole, up_dev, self.main(slot))
            self.put(slot, self.whole, down_dev, self.main(slot))
            self.put(slot, self.a, across_dev, self.main(slot))
            self.put(slot, self.whole, core_dev, self.main(slot))

        def own_across(self):
            slot = (y, z, c)
            self.put(slot, self.b, across_dev, self.late(slot))

        def round(self, yy, d, rows, kind):
            cut = (rows[0], rows[1] // 2), (rows[0] + rows[1] // 2, rows[1] // 2)
            if d == 4:
                slot = (yy, at_z(4), c)
                self.got(slot, cut[0], self.main(slot))
                self.got(slot, cut[1], self.half.at[kind])
                arrived = [slot]
            else:
                arrived = []
                for part, step, onward in ((0, 1, up_dev), (1, -1, down_dev)):
                    slot = (yy, at_z(-step * d), c)
                    self.got(slot, rows, self.main(slot))
                    if d < 3:
                        self.put(slot, rows, onward, self.main(slot))
                    else:
                        recv = self.half.at[kind] if part else self.main(slot)
                        self.put(slot, cut[part], onward, recv)
                    arrived.append(slot)
            for slot in arrived:
                if kind == 0:
                    self.put(slot, self.b, across_dev, self.late(slot))
                self.put(slot, rows, core_dev, self.main(slot))

        def plane(self, d):
            self.round(y, d, self.whole, 0)

        def other(self, d):
            self.round(oy, d, self.a, 1)

        def other_start(self):
            slot = (oy, z, c)
            self.got(slot, self.a, self.main(slot))
            self.put(slot, self.a, up_dev, self.main(slot))
            self.put(slot, self.a, down_dev, self.main(slot))
            self.put(slot, self.a, core_dev, self.main(slot))

        def places(self, d):
            return [at_z(d)] if d in (0, 4) else [at_z(-d), at_z(d)]

        def cross(self, d):
            for zz in self.places(d):
                slot = (oy, zz, c)
                self.got(slot, self.b, self.late(slot))
                self.put(slot, self.b, core_dev, self.late(slot))

        def chips(self, d):
            for zz in self.places(d):
                slot = (y, zz, oc)
                self.got(slot, self.whole, self.main(slot))
            return [(y, zz) for zz in self.places(d)]

        def other_chips(self, d):
            for zz in self.places(d):
                slot = (oy, zz, oc)
                self.got(slot, self.a, self.main(slot))
                self.got(slot, self.b, self.late(slot))
            return [(oy, zz) for zz in self.places(d)]

        def finish(self):
            for copy in self.sent:
                copy.wait_send()

    class HeadRing:
        def __init__(self, buf, sems):
            self.buf = buf
            self.recv, self.half, self.send = sems
            self.size = buf.shape[1]
            self.sent = []

        def desc(self, slot, rows, device, recv, index=0):
            view = self.buf.at[slot, pl.ds(*rows)]
            return pltpu.make_async_remote_copy(
                src_ref=view, dst_ref=view, send_sem=self.send.at[index], recv_sem=recv,
                device_id=device, device_id_type=MESH,
            )

        def put(self, slot, rows, step, recv, swap=False):
            device = (me, x * 2 + olow) if swap else (me, at_x(step) * 2 + low)
            copy = self.desc(slot, rows, device, recv, len(self.sent))
            copy.start()
            self.sent.append(copy)

        def got(self, slot, rows, recv):
            self.desc(slot, rows, (me, x * 2 + olow), recv).wait_recv()

        def start(self):
            whole = (0, self.size)
            for step in (1, -1):
                self.put(head, whole, step, self.recv.at[head])
            self.put(head, whole, 0, self.recv.at[head], swap=True)

        def pair(self):
            whole, slot = (0, self.size), x * 2 + olow
            self.got(slot, whole, self.recv.at[slot])
            for step in (1, -1):
                self.put(slot, whole, step, self.recv.at[slot])

        def one(self, kind):
            half = self.size // 2
            ll = olow if kind else low
            for part, step in ((0, 1), (1, -1)):
                slot = at_x(-step) * 2 + ll
                self.got(slot, (0, self.size), self.recv.at[slot])
                recv = self.half.at[kind] if part else self.recv.at[slot]
                self.put(slot, (part * half, half), step, recv)

        def two(self, kind):
            half = self.size // 2
            slot = at_x(2) * 2 + (olow if kind else low)
            self.got(slot, (0, half), self.recv.at[slot])
            self.got(slot, (half, half), self.half.at[kind])

        def finish(self):
            for copy in self.sent:
                copy.wait_send()

    qa_ring = Ring(qa_all, qa_sems, 96)
    qb_ring = Ring(qb_all, qb_sems, 96)
    kvring = Ring(kv_all, kv_sems, 96)
    vring = Ring(v_all, v_sems, 64)
    oring = HeadRing(wo, wo_sems)
    sring = HeadRing(s_all, s_sems)
    def a_copy(o):
        peer = rem(head + o, 8)
        return pltpu.make_async_remote_copy(
            src_ref=wo_own.at[:, peer], dst_ref=wo_mid.at[head],
            send_sem=a_send.at[o], recv_sem=a_recv.at[head],
            device_id=(me, peer), device_id_type=MESH,
        )

    def a_arrival(o):
        peer = rem(head + o, 8)
        return pltpu.make_async_remote_copy(
            src_ref=wo_own.at[:, peer], dst_ref=wo_mid.at[peer],
            send_sem=a_send.at[o], recv_sem=a_recv.at[peer],
            device_id=(me, peer), device_id_type=MESH,
        )

    a_local = pltpu.make_async_copy(wo_own.at[:, head], wo_mid.at[head], local_sem.at[6])

    loop(8, lambda o: a_copy(o).start())
    a_local.start()
    qa_ring.start()
    qb_ring.start()
    sring.start()

    for k in range(3):
        tell(token_sem.at[2 * k], up_dev)
        tell(token_sem.at[2 * k + 1], down_dev)
        pl.semaphore_wait(token_sem.at[2 * k], 1)
        pl.semaphore_wait(token_sem.at[2 * k + 1], 1)
    tell(token_sem.at[6], across_dev)
    pl.semaphore_wait(token_sem.at[6], 1)
    tell(token_sem.at[7], core_dev)
    pl.semaphore_wait(token_sem.at[7], 1)

    loop(8, lambda o: a_arrival(o).wait_recv())
    a_local.wait()

    def b_copy(o):
        peer = rem(me + o, 32)
        return pltpu.make_async_remote_copy(
            src_ref=wo_mid.at[peer // 4, rem(peer, 4)], dst_ref=wo.at[head, me],
            send_sem=b_send.at[o], recv_sem=b_recv.at[me],
            device_id=(peer, head), device_id_type=MESH,
        )

    def b_arrival(o):
        peer = rem(me + o, 32)
        return pltpu.make_async_remote_copy(
            src_ref=wo_mid.at[peer // 4, rem(peer, 4)], dst_ref=wo.at[head, peer],
            send_sem=b_send.at[o], recv_sem=b_recv.at[peer],
            device_id=(peer, head), device_id_type=MESH,
        )

    b_local = pltpu.make_async_copy(
        wo_mid.at[me // 4, rem(me, 4)], wo.at[head, me], local_sem.at[7]
    )
    loop(32, lambda o: b_copy(o).start())
    b_local.start()

    loads[4].wait()

    def add_squares(k, total):
        part = resid[:, pl.ds(pl.multiple_of(k * 512, 512), 512)].astype(jnp.float32)
        part = part * part
        return total + part[:, :128] + part[:, 128:256] + part[:, 256:384] + part[:, 384:]

    squares = lax.fori_loop(0, 16, add_squares, jnp.zeros((256, 128), jnp.float32))
    inv_ref[...] = lax.rsqrt(jnp.sum(squares, axis=1, keepdims=True) * (1.0 / 8192) + epsilon)

    acc[...] = jnp.zeros_like(acc)
    acc_kv[...] = jnp.zeros_like(acc_kv)
    acc_v[...] = jnp.zeros_like(acc_v)
    row = lax.broadcasted_iota(jnp.int32, (256, 256), 0)
    col = lax.broadcasted_iota(jnp.int32, (256, 256), 1)

    def column(values):
        return jnp.sum(jnp.where(row == col, values, 0.0), axis=1, keepdims=True)

    def project(chips, pairs):
        for yy, zz in chips:
            at = pl.multiple_of((yy * 8 + zz) * 512, 512)
            part = resid[:, pl.ds(at, 512)].astype(jnp.float32)
            normed = (part * inv_ref[...] * gain_ref[:, pl.ds(at, 512)]).astype(jnp.bfloat16)
            for weights, total, cols in pairs:
                total[:, cols] += jnp.dot(
                    normed, weights[yy, zz].reshape(512, 256), preferred_element_type=jnp.float32
                )

    left, right = pl.ds(0, 256), pl.ds(256, 256)

    def virtual_part(chips):
        for yy, zz in chips:
            for cc in range(2):
                j = seq_of(yy, zz, cc)
                gain = column(gain_ref[:, pl.ds(pl.multiple_of(j * 256, 256), 256)])
                for weights, cols in ((qa_all, left), (qb_all, right)):
                    scaled = (weights[yy, zz, cc].astype(jnp.float32) * gain).astype(jnp.bfloat16)
                    acc_v[:, cols] += jnp.dot(
                        wo[:, j].reshape(128, 256), scaled, preferred_element_type=jnp.float32
                    )

    def patch(chips):
        for yy, zz in chips:
            k = yy * 8 + zz
            rows = s_all[k // 2, :, pl.ds(pl.multiple_of(rem(k, 2) * 256, 256), 256)]
            acc[...] += inv_ref[...] * jnp.dot(
                rows, v_all[yy, zz].reshape(256, 512), preferred_element_type=jnp.float32
            )

    class Both:
        def __getattr__(self, name):
            def call(*args):
                getattr(qa_ring, name)(*args)
                return getattr(qb_ring, name)(*args)

            return call

    qring = Both()

    def take_q(chips):
        project(chips, ((qa_all, acc, left), (qb_all, acc, right)))
        return chips

    def take_kv(chips):
        project(chips, ((kv_all, acc_kv, left),))

    waiting = []
    qring.plane(1)
    loop(32, lambda o: b_arrival(o).wait_recv())
    b_local.wait()
    oring.start()
    qring.own_across()
    waiting += take_q(qring.chips(0))
    qring.plane(2)
    qring.other_start()
    waiting += take_q(qring.chips(1))
    sring.pair()
    oring.one(0)
    qring.plane(3)
    for k in (2, 3):
        loads[k].wait()
    kvring.start()
    kvring.own_across()
    oring.pair()
    qring.other(1)
    sring.one(0)
    waiting += take_q(qring.chips(2))
    qring.plane(4)
    kvring.plane(1)
    qring.other(2)
    waiting += take_q(qring.chips(3))
    oring.one(1)
    sring.one(1)
    kvring.plane(2)
    qring.cross(0)
    qring.cross(1)
    qring.other(3)
    waiting += take_q(qring.chips(4))
    oring.two(0)
    kvring.other_start()
    oring.two(1)
    virtual_part(waiting)
    kvring.plane(3)
    qring.cross(2)
    qring.other(4)
    for d in (0, 1, 2):
        virtual_part(take_q(qring.other_chips(d)))
    qring.cross(3)
    qring.cross(4)
    for d in (3, 4):
        virtual_part(take_q(qring.other_chips(d)))

    for r in range(4):
        cols = pl.ds(r * 128, 128)
        keep = edge_ref[me, head * 4 + r].astype(jnp.float32)
        v_all[y, z, c, :, cols] = (acc_v[:, cols] * keep).astype(jnp.bfloat16)
    vring.start()
    vring.own_across()
    kvring.other(1)
    for d in (0, 1, 2):
        take_kv(kvring.chips(d))
    vring.plane(1)
    kvring.plane(4)
    vring.other_start()
    kvring.other(2)
    vring.plane(2)
    for d in (3, 4):
        take_kv(kvring.chips(d))
    sring.two(0)
    sring.two(1)
    patch(vring.chips(0))
    kvring.other(3)
    vring.other(1)
    vring.plane(3)
    patch(vring.chips(1))
    kvring.other(4)
    vring.other(2)
    vring.plane(4)
    for d in range(5):
        kvring.cross(d)
    vring.cross(0)
    vring.cross(1)
    vring.other(3)
    patch(vring.chips(2))
    for d in range(5):
        take_kv(kvring.other_chips(d))
    patch(vring.other_chips(0))
    vring.cross(2)
    vring.other(4)
    patch(vring.chips(3))
    vring.cross(3)
    vring.cross(4)
    patch(vring.chips(4))
    keys = acc_kv[:, :128].astype(jnp.bfloat16)
    values = acc_kv[:, 128:].astype(jnp.bfloat16)
    for d in range(1, 5):
        patch(vring.other_chips(d))

    doc_row = doc_ref[...].astype(jnp.float32)
    allowed = (column(doc_row) == doc_row) & (col <= row)
    for r in range(4):
        cols = pl.ds(r * 128, 128)
        query = acc[:, cols].astype(jnp.bfloat16)
        scores = lax.dot_general(
            query, keys, (((1,), (1,)), ((), ())), preferred_element_type=jnp.float32
        ) * HEAD_SIZE ** (-0.5)
        scores = jnp.where(allowed, scores, -jnp.inf)
        weights = jnp.exp(scores - jnp.max(scores, axis=1, keepdims=True))
        weights = (weights / jnp.sum(weights, axis=1, keepdims=True)).astype(jnp.bfloat16)
        out_ref[:, cols] = jnp.dot(
            weights, values, preferred_element_type=jnp.float32
        ).astype(jnp.bfloat16)

    for ring in (qa_ring, qb_ring, kvring, vring, oring, sring):
        ring.finish()
    loop(8, lambda o: a_copy(o).wait_send())
    loop(32, lambda o: b_copy(o).wait_send())


def local(resid, norm_gain, sender_diff, w_out1, w_query, w_key, w_value, edge_mask, doc_ids):
    dma = pltpu.SemaphoreType.DMA
    anywhere = pl.BlockSpec(memory_space=pl.ANY)
    vmem = pl.BlockSpec(memory_space=pltpu.VMEM)
    smem = pl.BlockSpec(memory_space=pltpu.SMEM)
    bf16, f32 = jnp.bfloat16, jnp.float32
    return pl.pallas_call(
        kernel,
        out_shape=jax.ShapeDtypeStruct((256, 512), bf16),
        in_specs=[
            anywhere, vmem, anywhere, anywhere, anywhere, anywhere, anywhere, smem, vmem,
        ],
        out_specs=vmem,
        scratch_shapes=[
            pltpu.VMEM((256, 8192), bf16),
            pltpu.VMEM((2, NZ, 2, 256, 256), bf16),
            pltpu.VMEM((2, NZ, 2, 256, 256), bf16),
            pltpu.VMEM((2, NZ, 2, 256, 256), bf16),
            pltpu.VMEM((2, NZ, 2, 128, 512), bf16),
            pltpu.VMEM((8, 256, 512), bf16),
            pltpu.VMEM((8, 32, 16, 256), bf16),
            pltpu.VMEM((4, 8, 16, 256), bf16),
            pltpu.VMEM((8, 4, 16, 256), bf16),
            pltpu.VMEM((256, 512), f32),
            pltpu.VMEM((256, 256), f32),
            pltpu.VMEM((128, 512), f32),
            pltpu.VMEM((256, 1), f32),
            dma((9,)),
            pltpu.SemaphoreType.REGULAR((8,)),
            *[[dma((32,)), dma((32,)), dma((2,)), dma((52,))] for _ in range(4)],
            *[[dma((8,)), dma((2,)), dma((10,))] for _ in range(2)],
            dma((8,)), dma((8,)),
            dma((32,)), dma((32,)),
        ],
        compiler_params=pltpu.CompilerParams(
            collective_id=0, has_side_effects=True, vmem_limit_bytes=60 * 1024 * 1024
        ),
        name="patch_layer",
    )(
        resid,
        norm_gain.reshape(1, -1),
        sender_diff,
        w_out1.reshape(4, 8, 16, 256),
        w_query,
        w_key,
        w_value,
        edge_mask,
        doc_ids,
    )


def solution(mesh):
    placed = (
        P("seq", None),
        P(),
        P("seq", "head"),
        P("head", "seq"),
        P("seq", "head"),
        P("seq", "head"),
        P("seq", "head"),
        P(),
        P("seq", None),
    )
    return jax.shard_map(
        local, mesh=mesh, in_specs=placed, out_specs=P("seq", "head"), check_vma=False
    )
```
